32 devices in a mesh: groups: 2 (over y), tm: 4 (over z), head: 4 (over x, core).
Axes of the slice: x: 2, y: 2, z: 4, core: 2. Of those that a mesh axis runs over, the one named last changes fastest.
Arguments:
- queries: bfloat16 [8, 256, 3072], P(('groups', 'tm'), 'head'), parts along dimension 0, may hold values from -128 to 128
- keys: bfloat16 [8, 256, 3072], P(('groups', 'tm'), 'head'), parts along dimension 0, may hold values from -6 to 6
- values: bfloat16 [8, 256, 3072], P(('groups', 'tm'), 'head'), parts along dimension 0, may hold values from -6 to 6
- residual: bfloat16 [8, 256, 5120], P(('groups', 'tm'), None, 'head'), parts along dimension 0, may hold values from -3 to 3
- fresh_frame: bfloat16 [512, 5120], P('groups', 'head'), parts along dimension 0, may hold values from -6 to 6
- out_weight: bfloat16 [3072, 5120], P('tm', 'head'), may hold values from -0.875 to 0.875
- time_weight: bfloat16 [256, 5120], P(None, 'head'), may hold values from -0.375 to 0.375
- noise_steps: int32 [8], P(('groups', 'tm')), parts along dimension 0, may hold values from 0 to 49, as said below
- frame_mask: int32 [8, 4], P(('groups', 'tm')), parts along dimension 0, may hold values from 0 to 1, as said below
Outputs:
- rolled: bfloat16 [8, 256, 5120], P(('groups', 'tm'), None, 'head'), parts along dimension 0
The draws below stay inside these ranges and needn't reach their ends.
There are 2 independent parts, one for each index of `groups`. The reference program is written for one: setup_inputs(seed, part) draws one part's arguments, and reference() takes and returns one part's arrays. A program takes and returns all parts, laid end to end along the dimension named above; an argument that names none is the same for every part. Nothing has to cross between parts.
Inputs may be any that keep to these rules, and one draw needn't show every extreme that they name: frame_mask[i, j] is 1 exactly for i - L_i < j <= i, with a whole number L_i from 1 to 4 for each frame i; the last frame has L_i = 4. `noise_steps`: never falling along the frames; the first frame has 0 and the last 49.
All inputs are finite; a program needn't handle non-finite values.
Results may differ from the reference program's by a relative error of at most 0.0065.
Values may be sent and summed in bfloat16 or wider, within the bound.
A program may use at most 64 MiB of HBM per device.

```python
import math
import jax
import jax.numpy as jnp
from jax import lax

D = 5120
HD = 128
HEADS = 24
FREQ = 256
STEPS = 50
TOK = 256
FRAMES = 4
WIN = 4


def draw_pair(key):
    base = jax.random.fold_in(key, 11)
    key_normal, key_query = jax.random.split(base, 2)
    shape = (FRAMES, TOK, HEADS * HD)
    keys_raw = jnp.clip(jax.random.normal(key_normal, shape, jnp.float32), -6.0, 6.0)
    query_raw = jnp.clip(2.0 * jax.random.normal(key_query, shape, jnp.float32), -12.0, 12.0)
    return (query_raw, keys_raw)


def draw_queries(key, part):
    return draw_pair(key)[0].astype(jnp.bfloat16)


def draw_keys(key, part):
    return draw_pair(key)[1].astype(jnp.bfloat16)


def draw_noise_steps(key, part):
    picks = jax.random.randint(jax.random.fold_in(key, 23), (FRAMES,), 0, STEPS)
    ordered = jnp.sort(picks)
    position = jnp.arange(FRAMES)
    ordered = jnp.where(position == 0, 0, jnp.where(position == FRAMES - 1, STEPS - 1, ordered))
    return ordered.astype(jnp.int32)


def draw_frame_mask(key, part):
    spans = jax.random.randint(jax.random.fold_in(key, 31), (FRAMES,), 1, WIN + 1)
    position = jnp.arange(FRAMES)
    spans = jnp.where(position == FRAMES - 1, WIN, spans)
    spans = jnp.minimum(spans, position + 1)
    rows = position[:, None]
    cols = position[None, :]
    return ((cols <= rows) & (cols > rows - spans[:, None])).astype(jnp.int32)


def steps_of(stream_key, dims, cuts, least, high):
    factor_of, own = 1.0, jax.random.fold_in(stream_key, 6)
    for dim, shards_of in cuts:
        draws = jnp.exp(jax.random.uniform(jax.random.fold_in(own, dim), (shards_of,), jnp.float32, least / len(cuts), high / len(cuts)))
        factor_of = factor_of * jnp.repeat(draws, dims[dim] // shards_of).reshape([-1 if axis == dim else 1 for axis in range(len(dims))])
    return factor_of


def scatter_about(key, dims, scale, reach, cuts=(), kind=jnp.bfloat16):
    gain = steps_of(key, dims, cuts, -0.22, 0.18) if cuts else 1.0
    drawn = jax.random.normal(key, dims, jnp.float32) * scale * gain
    return jnp.minimum(jnp.maximum(drawn, -reach), reach).astype(kind)


def setup_inputs(seed: int = 0, part: int = 0) -> dict:
    arg_keys = jax.random.split(jax.random.key(seed), 10)
    part_splits = jax.random.split(jax.random.fold_in(arg_keys[9], part), 10)
    queries = draw_queries(jax.random.fold_in(jax.random.fold_in(arg_keys[9], part), 71), part)
    keys = draw_keys(jax.random.fold_in(jax.random.fold_in(arg_keys[9], part), 71), part)
    values = scatter_about(part_splits[2], (FRAMES, TOK, HEADS * HD), 1.0, 6.0, ((0, 4), (1, 4)))
    residual = scatter_about(part_splits[3], (FRAMES, TOK, D), 0.5, 3.0, ((0, 4), (2, 4)))
    fresh_frame = scatter_about(part_splits[4], (TOK, D), 1.0, 6.0, ((1, 4),))
    out_weight = scatter_about(arg_keys[5], (HEADS * HD, D), (HEADS * HD // 64) ** -0.5, 0.875, ((0, 4), (1, 4)))
    time_weight = scatter_about(arg_keys[6], (FREQ, D), FREQ ** -0.5, 0.375, ((1, 4),))
    noise_steps = draw_noise_steps(jax.random.fold_in(jax.random.fold_in(arg_keys[9], part), 71), part)
    frame_mask = draw_frame_mask(jax.random.fold_in(jax.random.fold_in(arg_keys[9], part), 71), part)
    return dict(queries=queries, keys=keys, values=values, residual=residual, fresh_frame=fresh_frame, out_weight=out_weight, time_weight=time_weight, noise_steps=noise_steps, frame_mask=frame_mask)


def time_features(noise_steps):
    timestep = 1000.0 * (noise_steps.astype(jnp.float32) + 1.0) / STEPS
    half = FREQ // 2
    rates = jnp.exp(-math.log(10000.0) * jnp.arange(half).astype(jnp.float32) / half)
    angles = timestep[:, None] * rates[None, :]
    return jnp.concatenate([jnp.cos(angles), jnp.sin(angles)], axis=1)

def reference(queries, keys, values, residual, fresh_frame, out_weight, time_weight, noise_steps, frame_mask):
    width = HEADS * HD
    scale = 1.0 / math.sqrt(HD)
    blank = jnp.zeros((WIN - 1, TOK, width), keys.dtype)
    keys_padded = jnp.concatenate([blank, keys], axis=0)
    values_padded = jnp.concatenate([blank, values], axis=0)
    mask_padded = jnp.concatenate([jnp.zeros((FRAMES, WIN - 1), jnp.int32), frame_mask.astype(jnp.int32)], axis=1)

    def one_frame(frame):
        query_rows = lax.dynamic_index_in_dim(queries, frame, 0, keepdims=False).astype(jnp.float32).reshape(TOK, HEADS, HD)
        key_rows = lax.dynamic_slice_in_dim(keys_padded, frame, WIN, 0).astype(jnp.float32).reshape(WIN * TOK, HEADS, HD)
        value_rows = lax.dynamic_slice_in_dim(values_padded, frame, WIN, 0).astype(jnp.float32).reshape(WIN * TOK, HEADS, HD)
        mask_row = lax.dynamic_index_in_dim(mask_padded, frame, 0, keepdims=False)
        allowed = jnp.repeat(lax.dynamic_slice_in_dim(mask_row, frame, WIN, 0), TOK)
        scores = jnp.einsum('qhd,khd->hqk', query_rows, key_rows) * scale
        scores = jnp.where(allowed[None, None, :] > 0, scores, -1e+30)
        peak = lax.optimization_barrier(jnp.max(scores, axis=2, keepdims=True))
        lifted = jnp.exp(scores - peak)
        totals = lax.optimization_barrier(jnp.sum(lifted, axis=2))
        rounded = lax.optimization_barrier(lifted.astype(jnp.bfloat16)).astype(jnp.float32)
        mixed = jnp.einsum('hqk,khd->qhd', rounded, value_rows) / jnp.transpose(totals)[:, :, None]
        return mixed.reshape(TOK, width).astype(jnp.bfloat16)
    attention = lax.map(one_frame, jnp.arange(FRAMES, dtype=jnp.int32))
    projected = jnp.dot(attention.reshape(FRAMES * TOK, width), out_weight, preferred_element_type=jnp.float32).reshape(FRAMES, TOK, D)
    gate = jnp.dot(time_features(noise_steps), time_weight.astype(jnp.float32), precision=lax.Precision.HIGHEST)
    updated = (residual.astype(jnp.float32) + gate[:, None, :] * projected).astype(jnp.bfloat16)
    return jnp.concatenate([updated[1:], fresh_frame[None]], axis=0)
```

```python
import functools
import math

import jax
import jax.numpy as jnp
from jax import lax
from jax.experimental import pallas as pl
from jax.experimental.pallas import tpu as pltpu
from jax.sharding import PartitionSpec as P

HD = 128
FREQ = 256
STEPS = 50


def shifted(value, axis, steps):
    count = lax.axis_size(axis)
    leading, last = (max(0, -steps), min(count, count - steps))
    return lax.ppermute(value, axis, [(source, source + steps) for source in range(leading, last)])


def time_features(noise_steps):
    timestep = 1000.0 * (noise_steps.astype(jnp.float32) + 1.0) / STEPS
    half = FREQ // 2
    rates = jnp.exp(-math.log(10000.0) * jnp.arange(half).astype(jnp.float32) / half)
    angles = timestep[:, None] * rates[None, :]
    return jnp.concatenate([jnp.cos(angles), jnp.sin(angles)], axis=1)


def on_device(
    queries, keys, values, residual, fresh_frame, out_weight, time_weight, noise_steps, frame_mask
):
    query_local, key_local, value_local = (
        lax.all_to_all(queries, "head", split_axis=2, concat_axis=1, tiled=True),
        lax.all_to_all(keys, "head", split_axis=2, concat_axis=1, tiled=True),
        lax.all_to_all(values, "head", split_axis=2, concat_axis=1, tiled=True),
    )
    tokens = query_local.shape[1]
    heads_here = query_local.shape[2] // HD
    scale = 1.0 / math.sqrt(HD)
    query_heads = query_local[0].reshape(tokens, heads_here, HD)
    key_value = jnp.stack([key_local[0], value_local[0]], axis=0)
    frame = lax.axis_index("tm")
    frames_total = lax.axis_size("tm")
    window = min(8, frames_total)
    mask_row = frame_mask[0]
    columns = jnp.arange(mask_row.shape[0], dtype=jnp.int32)

    def allowed_at(offset):
        hits = jnp.sum(jnp.where(columns == frame - offset, mask_row, 0))
        return hits > 0

    def absorb(state, block, allowed):
        running_max, weight_sum, accumulated = state
        key_heads = block[0].reshape(tokens, heads_here, HD)
        value_heads = block[1].reshape(tokens, heads_here, HD)
        scores = (
            jnp.einsum("qhd,khd->hqk", query_heads, key_heads, preferred_element_type=jnp.float32)
            * scale
        )
        new_max = jnp.where(allowed, jnp.maximum(running_max, jnp.max(scores, axis=2)), running_max)
        lifted = jnp.where(allowed, jnp.exp(jnp.minimum(scores - new_max[:, :, None], 0.0)), 0.0)
        factor = jnp.exp(running_max - new_max)
        weight_sum = weight_sum * factor + jnp.sum(lifted, axis=2)
        rounded = lifted.astype(jnp.bfloat16)
        accumulated = accumulated * jnp.transpose(factor)[:, :, None] + jnp.einsum(
            "hqk,khd->qhd", rounded, value_heads, preferred_element_type=jnp.float32
        )
        return (new_max, weight_sum, accumulated)

    state = (
        jnp.full((heads_here, tokens), -1e30, jnp.float32),
        jnp.zeros((heads_here, tokens), jnp.float32),
        jnp.zeros((tokens, heads_here, HD), jnp.float32),
    )
    state = absorb(state, key_value, allowed_at(0))
    moving = key_value
    for offset in range(1, window):
        moving = shifted(moving, "tm", 1)
        state = absorb(state, moving, allowed_at(offset))
    running_max, weight_sum, accumulated = state
    attention = (
        (accumulated / jnp.transpose(weight_sum)[:, :, None])
        .reshape(tokens, heads_here * HD)
        .astype(jnp.bfloat16)
    )
    weight_cols = lax.all_gather(out_weight, "tm", axis=0, tiled=True)
    projected = jnp.dot(
        lax.all_gather(attention, "head", axis=1, tiled=True),
        weight_cols,
        preferred_element_type=jnp.float32,
    )
    gate = jnp.dot(
        time_features(noise_steps), time_weight.astype(jnp.float32), precision=lax.Precision.HIGHEST
    )
    updated = (residual[0].astype(jnp.float32) + gate * projected).astype(jnp.bfloat16)
    moved = shifted(updated, "tm", -1)
    rolled = jnp.where(frame == frames_total - 1, fresh_frame, moved)
    return rolled[None]


def fused_kernel(
    T, G, C, hp, pieces,
    q_ref, k_ref, v_ref, res_ref, fresh_ref, w_ref, meta_ref,
    out_ref,
    qb, kb, vb, ab, mb, wb, rb, pb, down_out, down_in, up_out, up_in,
    load_sem, meta_send, meta_recv, qkv_send, qkv_recv, pass_send, pass_recv,
    ax_send, ax_recv, ac_send, ac_recv, dn_send, dn_recv, up_send, up_recv,
):
    t = lax.axis_index("tm")
    h = lax.axis_index("head")
    x = h // C
    c = lax.rem(h, C)
    H = G * C
    tl = q_ref.shape[1]
    cw = hp * HD
    tokens = tl * H
    half = G * tl
    nb = w_ref.shape[1] // pieces
    gate_rows = w_ref.shape[1] // HD

    def to(tt, hh):
        return dict(device_id={"tm": tt, "head": hh}, device_id_type=pl.DeviceIdType.MESH)

    def landed(ref, sem):
        pltpu.make_async_copy(ref, ref, sem).wait()

    others = [(dt, dx) for dt in range(T) for dx in reversed(range(G)) if (dt, dx) != (0, 0)]

    loads = [
        pltpu.make_async_copy(w_ref, wb, load_sem.at[0]),
        pltpu.make_async_copy(res_ref.at[0], rb, load_sem.at[1]),
    ]
    for copy in loads:
        copy.start()

    barrier = pltpu.get_barrier_semaphore()
    for dt, dx in others:
        pl.semaphore_signal(
            barrier, inc=1, **to(lax.rem(t + dt, T), lax.rem(x + dx, G) * C + c)
        )
    for dc in range(1, C):
        pl.semaphore_signal(barrier, inc=1, **to(t, x * C + lax.rem(c + dc, C)))
    pl.semaphore_wait(barrier, len(others) + C - 1)

    own_meta = pltpu.make_async_copy(meta_ref, mb.at[t], meta_recv.at[t])
    own_meta.start()
    meta_copies = []
    for dt in range(1, T):
        meta_copies.append(
            pltpu.make_async_remote_copy(
                src_ref=meta_ref, dst_ref=mb.at[t], send_sem=meta_send.at[dt],
                recv_sem=meta_recv.at[t], **to(lax.rem(t + dt, T), h),
            )
        )
        meta_copies[-1].start()

    sources = ((q_ref, qb), (k_ref, kb), (v_ref, vb))

    def slot(kind, f, xs):
        return qb.at[f, xs] if kind == 0 else sources[kind][1].at[f, xs * C + c]

    def block(kind, tt, xx):
        column = pl.multiple_of((tt * G + xx) * cw, HD)
        return sources[kind][0].at[0, :, pl.ds(column, cw)]

    def outgoing(kind, dt, dx):
        tt, xx = lax.rem(t + dt, T), lax.rem(x + dx, G)
        return pltpu.make_async_remote_copy(
            src_ref=block(kind, tt, xx), dst_ref=slot(kind, t, x),
            send_sem=qkv_send.at[kind, dt, dx], recv_sem=qkv_recv.at[kind, t, x],
            **to(tt, xx * C + c),
        )

    def own(kind):
        return pltpu.make_async_copy(block(kind, t, x), slot(kind, t, x), qkv_recv.at[kind, t, x])

    for dt, dx in others:
        for kind in (1, 2):
            outgoing(kind, dt, dx).start()

        @pl.when(t > 0)
        def _():
            outgoing(0, dt, dx).start()

    for kind in (1, 2):
        own(kind).start()

    @pl.when(t > 0)
    def _():
        own(0).start()

    def passed(kind, dc, f, xs):
        return pltpu.make_async_remote_copy(
            src_ref=slot(kind, f, xs), dst_ref=slot(kind, f, xs),
            send_sem=pass_send.at[kind - 1, dc, f, xs], recv_sem=pass_recv.at[kind - 1, dc, f, xs],
            **to(t, x * C + lax.rem(c + dc, C)),
        )

    for dt in range(T):
        for dx in range(G):
            f, xs = lax.rem(t + dt, T), lax.rem(x + dx, G)
            for kind in (1, 2):
                landed(slot(kind, f, xs), qkv_recv.at[kind, f, xs])
                for dc in range(1, C):
                    passed(kind, dc, f, xs).start()
    for f in range(T):
        for xs in range(G):
            if f > 0:
                landed(slot(0, f, xs), qkv_recv.at[0, f, xs])
            for kind in (1, 2):
                for dc in range(1, C):
                    from_c = xs * C + lax.rem(c + C - dc, C)
                    landed(sources[kind][1].at[f, from_c], pass_recv.at[kind - 1, dc, f, xs])
        landed(mb.at[f], meta_recv.at[f])
    for copy in loads:
        copy.wait()

    def across(r, dx):
        xx = lax.rem(x + dx, G)
        return pltpu.make_async_remote_copy(
            src_ref=ab.at[x, r, c], dst_ref=ab.at[x, r, c],
            send_sem=ax_send.at[r, dx], recv_sem=ax_recv.at[r, dx],
            **to(t, xx * C + c),
        )

    def aside(r, dx, dc):
        xs = lax.rem(x + dx, G)
        return pltpu.make_async_remote_copy(
            src_ref=ab.at[xs, r, c], dst_ref=ab.at[xs, r, c],
            send_sem=ac_send.at[r, dx, dc], recv_sem=ac_recv.at[r, dx, dc],
            **to(t, x * C + lax.rem(c + dc, C)),
        )

    scale = 1.0 / math.sqrt(HD)
    for r in range(T - 1):
        f = r + 1
        keys_here = (f + 1) * tokens
        allowed = jnp.concatenate(
            [
                jnp.broadcast_to(mb[f, gate_rows + g : gate_rows + g + 1, 0:1], (1, tokens))
                for g in range(f + 1)
            ],
            axis=1,
        )
        for j in range(hp):
            cols = slice(j * HD, (j + 1) * HD)
            query = qb[f, :, :, cols].reshape(half, HD)
            key = kb[0 : f + 1, :, :, cols].reshape(keys_here, HD)
            value = vb[0 : f + 1, :, :, cols].reshape(keys_here, HD)
            scores = (
                lax.dot_general(
                    query, key, (((1,), (1,)), ((), ())), preferred_element_type=jnp.float32
                )
                * scale
            )
            scores = jnp.where(allowed > 0.5, scores, -1e30)
            peak = jnp.max(scores, axis=1, keepdims=True)
            lifted = jnp.exp(scores - peak)
            total = jnp.sum(lifted, axis=1, keepdims=True)
            mixed = jnp.dot(
                lifted.astype(jnp.bfloat16), value, preferred_element_type=jnp.float32
            )
            ab[x, r, c, :, cols] = (mixed / total).astype(jnp.bfloat16)
        for dx in range(1, G):
            across(r, dx).start()
        for dc in range(1, C):
            aside(r, 0, dc).start()

    def down(r, p):
        return pltpu.make_async_remote_copy(
            src_ref=down_out.at[r, p], dst_ref=down_in.at[r, p],
            send_sem=dn_send.at[r, p], recv_sem=dn_recv.at[r, p], **to(t - 1, h),
        )

    def up(r, p):
        return pltpu.make_async_remote_copy(
            src_ref=up_out.at[r, p], dst_ref=up_in.at[r, p],
            send_sem=up_send.at[r, p], recv_sem=up_recv.at[r, p], **to(t + 1, h),
        )

    for r in range(T - 1):
        for dx in range(1, G):
            xs = lax.rem(x + G - dx, G)
            landed(ab.at[xs, r, c], ax_recv.at[r, dx])
            for dc in range(1, C):
                aside(r, G - dx, dc).start()
        for dx in range(G):
            for dc in range(1, C):
                xs, cs = lax.rem(x + dx, G), lax.rem(c + C - dc, C)
                landed(ab.at[xs, r, cs], ac_recv.at[r, dx, dc])
        for p in range(pieces):
            cols = slice(p * nb, (p + 1) * nb)
            gate = jnp.concatenate(
                [mb[r + 1, b : b + 1, :] for b in range(p * nb // HD, (p + 1) * nb // HD)], axis=1
            )
            partial = 0.0
            for xs in range(G):
                partial += jnp.dot(
                    ab[xs, r].reshape(tokens, cw),
                    wb[xs * cw : (xs + 1) * cw, cols],
                    preferred_element_type=jnp.float32,
                )
            pb[r, p] = partial * gate

            @pl.when(t == r + 1)
            def _():
                for cs in range(C):
                    for xs in range(G):
                        rows = (cs * G + xs) * tl
                        token = (xs * C + cs) * tl
                        pb[r, p, rows : rows + tl, :] += rb[token : token + tl, cols].astype(
                            jnp.float32
                        )

            @pl.when(t == T - 1)
            def _():
                down_out[r, p] = pb[r, p].astype(jnp.bfloat16)
                down(r, p).start()

            if r > 0:

                @pl.when(t == 0)
                def _():
                    up_out[r, p] = pb[r, p].astype(jnp.bfloat16)
                    up(r, p).start()

    for r in reversed(range(2, T - 1)):
        for p in range(pieces):

            @pl.when((t > 0) & (t < r))
            def _():
                landed(up_in.at[r, p], up_recv.at[r, p])
                up_out[r, p] = (pb[r, p] + up_in[r, p].astype(jnp.float32)).astype(jnp.bfloat16)
                up(r, p).start()

    for r in range(T - 2):
        for p in range(pieces):

            @pl.when((t > r) & (t < T - 1))
            def _():
                landed(down_in.at[r, p], dn_recv.at[r, p])
                down_out[r, p] = (pb[r, p] + down_in[r, p].astype(jnp.float32)).astype(
                    jnp.bfloat16
                )
                down(r, p).start()

    for r in range(T - 1):

        @pl.when(t == r)
        def _():
            for p in range(pieces):
                cols = slice(p * nb, (p + 1) * nb)
                landed(down_in.at[r, p], dn_recv.at[r, p])
                if r > 0:
                    landed(up_in.at[r, p], up_recv.at[r, p])
                for cs in range(C):
                    for xs in range(G):
                        rows = slice((cs * G + xs) * tl, (cs * G + xs + 1) * tl)
                        token = (xs * C + cs) * tl
                        total = pb[r, p, rows, :] + down_in[r, p, rows, :].astype(jnp.float32)
                        if r > 0:
                            total += up_in[r, p, rows, :].astype(jnp.float32)
                        out_ref[token : token + tl, cols] = total.astype(out_ref.dtype)

    @pl.when(t == T - 1)
    def _():
        copy = pltpu.make_async_copy(fresh_ref, out_ref, load_sem.at[2])
        copy.start()
        copy.wait()

    for copy in meta_copies:
        copy.wait_send()
    for dt, dx in others:
        for kind in (1, 2):
            outgoing(kind, dt, dx).wait_send()

        @pl.when(t > 0)
        def _():
            outgoing(0, dt, dx).wait_send()

    for dc in range(1, C):
        for f in range(T):
            for xs in range(G):
                for kind in (1, 2):
                    passed(kind, dc, f, xs).wait_send()
    for r in range(T - 1):
        for dx in range(1, G):
            across(r, dx).wait_send()
        for dx in range(G):
            for dc in range(1, C):
                aside(r, dx, dc).wait_send()
        for p in range(pieces):

            @pl.when(t > r)
            def _():
                down(r, p).wait_send()

            @pl.when(t < r)
            def _():
                up(r, p).wait_send()


def fused(T, H, heads):
    def on_device_fused(
        queries, keys, values, residual, fresh_frame, out_weight, time_weight, noise_steps, frame_mask
    ):
        level_heads = heads // T
        G = math.gcd(level_heads, H)
        C = H // G
        hp = level_heads // G
        tl = queries.shape[1]
        tokens = tl * H
        width = out_weight.shape[1]
        pieces = 2
        nb = width // pieces
        gate = jnp.dot(
            time_features(noise_steps), time_weight.astype(jnp.float32), precision=lax.Precision.HIGHEST
        )
        gate_rows = width // HD
        meta_rows = -(-(gate_rows + T) // 8) * 8
        mask_rows = jnp.broadcast_to(frame_mask[0].astype(jnp.float32)[:, None], (T, HD))
        meta = jnp.concatenate(
            [
                gate.reshape(gate_rows, HD),
                mask_rows,
                jnp.zeros((meta_rows - gate_rows - T, HD), jnp.float32),
            ],
            axis=0,
        )
        cw = hp * HD
        bf16, f32 = jnp.bfloat16, jnp.float32
        dma = pltpu.SemaphoreType.DMA
        chunk = (T - 1, pieces, tokens, nb)
        out = pl.pallas_call(
            functools.partial(fused_kernel, T, G, C, hp, pieces),
            out_shape=jax.ShapeDtypeStruct((tokens, width), bf16),
            in_specs=[pl.BlockSpec(memory_space=pl.ANY)] * 7,
            out_specs=pl.BlockSpec(memory_space=pltpu.VMEM),
            scratch_shapes=[
                pltpu.VMEM((T, G, tl, cw), bf16),
                pltpu.VMEM((T, H, tl, cw), bf16),
                pltpu.VMEM((T, H, tl, cw), bf16),
                pltpu.VMEM((G, T - 1, C, G * tl, cw), bf16),
                pltpu.VMEM((T, meta_rows, HD), f32),
                pltpu.VMEM(out_weight.shape, bf16),
                pltpu.VMEM((tokens, width), bf16),
                pltpu.VMEM(chunk, f32),
                pltpu.VMEM(chunk, bf16),
                pltpu.VMEM(chunk, bf16),
                pltpu.VMEM(chunk, bf16),
                pltpu.VMEM(chunk, bf16),
                dma((3,)),
                dma((T,)),
                dma((T,)),
                dma((3, T, G)),
                dma((3, T, G)),
                dma((2, C, T, G)),
                dma((2, C, T, G)),
                dma((T - 1, G)),
                dma((T - 1, G)),
                dma((T - 1, G, C)),
                dma((T - 1, G, C)),
                dma((T - 1, pieces)),
                dma((T - 1, pieces)),
                dma((T - 1, pieces)),
                dma((T - 1, pieces)),
            ],
            compiler_params=pltpu.CompilerParams(
                collective_id=0, has_side_effects=True, vmem_limit_bytes=56 * 1024 * 1024
            ),
        )(queries, keys, values, residual, fresh_frame, out_weight, meta)
        return out[None]

    return on_device_fused


def solution(mesh):
    placed = (
        P(("groups", "tm"), "head", None),
        P(("groups", "tm"), "head", None),
        P(("groups", "tm"), "head", None),
        P(("groups", "tm"), None, "head"),
        P("groups", "head"),
        P("tm", "head"),
        P(None, "head"),
        P(("groups", "tm")),
        P(("groups", "tm"), None),
    )
    def whole(*args):
        frames, spread = mesh.shape["tm"], mesh.shape["head"]
        heads = args[0].shape[2] // HD
        fits = 1 < frames <= 4 and heads % frames == 0 and args[5].shape[1] % (spread * 2 * HD) == 0
        return jax.shard_map(
            fused(frames, spread, heads) if fits else on_device,
            mesh=mesh,
            in_specs=placed,
            out_specs=P(("groups", "tm"), None, "head"),
            check_vma=False,
        )(*args)

    return whole
```

```python
import functools
import math

import jax
import jax.numpy as jnp
from jax import lax
from jax.experimental import pallas as pl
from jax.experimental.pallas import tpu as pltpu
from jax.sharding import PartitionSpec as P

HD = 128
FREQ = 256
STEPS = 50


def shifted(value, axis, steps):
    count = lax.axis_size(axis)
    leading, last = (max(0, -steps), min(count, count - steps))
    return lax.ppermute(value, axis, [(source, source + steps) for source in range(leading, last)])


def time_features(noise_steps):
    timestep = 1000.0 * (noise_steps.astype(jnp.float32) + 1.0) / STEPS
    half = FREQ // 2
    rates = jnp.exp(-math.log(10000.0) * jnp.arange(half).astype(jnp.float32) / half)
    angles = timestep[:, None] * rates[None, :]
    return jnp.concatenate([jnp.cos(angles), jnp.sin(angles)], axis=1)


def on_device(
    queries, keys, values, residual, fresh_frame, out_weight, time_weight, noise_steps, frame_mask
):
    query_local, key_local, value_local = (
        lax.all_to_all(queries, "head", split_axis=2, concat_axis=1, tiled=True),
        lax.all_to_all(keys, "head", split_axis=2, concat_axis=1, tiled=True),
        lax.all_to_all(values, "head", split_axis=2, concat_axis=1, tiled=True),
    )
    tokens = query_local.shape[1]
    heads_here = query_local.shape[2] // HD
    scale = 1.0 / math.sqrt(HD)
    query_heads = query_local[0].reshape(tokens, heads_here, HD)
    key_value = jnp.stack([key_local[0], value_local[0]], axis=0)
    frame = lax.axis_index("tm")
    frames_total = lax.axis_size("tm")
    window = min(8, frames_total)
    mask_row = frame_mask[0]
    columns = jnp.arange(mask_row.shape[0], dtype=jnp.int32)

    def allowed_at(offset):
        hits = jnp.sum(jnp.where(columns == frame - offset, mask_row, 0))
        return hits > 0

    def absorb(state, block, allowed):
        running_max, weight_sum, accumulated = state
        key_heads = block[0].reshape(tokens, heads_here, HD)
        value_heads = block[1].reshape(tokens, heads_here, HD)
        scores = (
            jnp.einsum("qhd,khd->hqk", query_heads, key_heads, preferred_element_type=jnp.float32)
            * scale
        )
        new_max = jnp.where(allowed, jnp.maximum(running_max, jnp.max(scores, axis=2)), running_max)
        lifted = jnp.where(allowed, jnp.exp(jnp.minimum(scores - new_max[:, :, None], 0.0)), 0.0)
        factor = jnp.exp(running_max - new_max)
        weight_sum = weight_sum * factor + jnp.sum(lifted, axis=2)
        rounded = lifted.astype(jnp.bfloat16)
        accumulated = accumulated * jnp.transpose(factor)[:, :, None] + jnp.einsum(
            "hqk,khd->qhd", rounded, value_heads, preferred_element_type=jnp.float32
        )
        return (new_max, weight_sum, accumulated)

    state = (
        jnp.full((heads_here, tokens), -1e30, jnp.float32),
        jnp.zeros((heads_here, tokens), jnp.float32),
        jnp.zeros((tokens, heads_here, HD), jnp.float32),
    )
    state = absorb(state, key_value, allowed_at(0))
    moving = key_value
    for offset in range(1, window):
        moving = shifted(moving, "tm", 1)
        state = absorb(state, moving, allowed_at(offset))
    running_max, weight_sum, accumulated = state
    attention = (
        (accumulated / jnp.transpose(weight_sum)[:, :, None])
        .reshape(tokens, heads_here * HD)
        .astype(jnp.bfloat16)
    )
    weight_cols = lax.all_gather(out_weight, "tm", axis=0, tiled=True)
    projected = jnp.dot(
        lax.all_gather(attention, "head", axis=1, tiled=True),
        weight_cols,
        preferred_element_type=jnp.float32,
    )
    gate = jnp.dot(
        time_features(noise_steps), time_weight.astype(jnp.float32), precision=lax.Precision.HIGHEST
    )
    updated = (residual[0].astype(jnp.float32) + gate * projected).astype(jnp.bfloat16)
    moved = shifted(updated, "tm", -1)
    rolled = jnp.where(frame == frames_total - 1, fresh_frame, moved)
    return rolled[None]


def fused_kernel(
    T, G, C, hp, pieces,
    q_ref, k_ref, v_ref, res_ref, fresh_ref, w_ref, tw_ref, meta_ref,
    out_ref,
    qb, kb, vb, ab, mb, fb, gb, wb, twb, rb, pb, down_out, down_in, up_out, up_in,
    load_sem, meta_send, meta_recv, qkv_send, qkv_recv, pass_send, pass_recv,
    ax_send, ax_recv, ac_send, ac_recv, dn_send, dn_recv, up_send, up_recv,
):
    t = lax.axis_index("tm")
    h = lax.axis_index("head")
    x = h // C
    c = lax.rem(h, C)
    H = G * C
    tl = q_ref.shape[1]
    cw = hp * HD
    tokens = tl * H
    half = G * tl
    nb = w_ref.shape[1] // pieces
    mask_row = FREQ // HD

    def to(tt, hh):
        return dict(device_id={"tm": tt, "head": hh}, device_id_type=pl.DeviceIdType.MESH)

    def landed(ref, sem):
        pltpu.make_async_copy(ref, ref, sem).wait()

    others = [(dt, dx) for dt in range(T) for dx in reversed(range(G)) if (dt, dx) != (0, 0)]

    loads = [
        pltpu.make_async_copy(w_ref, wb, load_sem.at[0]),
        pltpu.make_async_copy(res_ref.at[0], rb, load_sem.at[1]),
        pltpu.make_async_copy(tw_ref, twb, load_sem.at[2]),
    ]
    for copy in loads:
        copy.start()

    barrier = pltpu.get_barrier_semaphore()
    for dt, dx in others:
        pl.semaphore_signal(
            barrier, inc=1, **to(lax.rem(t + dt, T), lax.rem(x + dx, G) * C + c)
        )
    for dc in range(1, C):
        pl.semaphore_signal(barrier, inc=1, **to(t, x * C + lax.rem(c + dc, C)))
    pl.semaphore_wait(barrier, len(others) + C - 1)

    own_meta = pltpu.make_async_copy(meta_ref, mb.at[t], meta_recv.at[t])
    own_meta.start()
    meta_copies = []
    for dt in range(1, T):
        meta_copies.append(
            pltpu.make_async_remote_copy(
                src_ref=meta_ref, dst_ref=mb.at[t], send_sem=meta_send.at[dt],
                recv_sem=meta_recv.at[t], **to(lax.rem(t + dt, T), h),
            )
        )
        meta_copies[-1].start()

    sources = ((q_ref, qb), (k_ref, kb), (v_ref, vb))

    def slot(kind, f, xs):
        return qb.at[f, xs] if kind == 0 else sources[kind][1].at[f, xs * C + c]

    def block(kind, tt, xx):
        column = pl.multiple_of((tt * G + xx) * cw, HD)
        return sources[kind][0].at[0, :, pl.ds(column, cw)]

    def outgoing(kind, tt, dx):
        xx = lax.rem(x + dx, G)
        return pltpu.make_async_remote_copy(
            src_ref=block(kind, tt, xx), dst_ref=slot(kind, t, x),
            send_sem=qkv_send.at[kind, tt, dx], recv_sem=qkv_recv.at[kind, t, x],
            **to(tt, xx * C + c),
        )

    def own(kind):
        return pltpu.make_async_copy(block(kind, t, x), slot(kind, t, x), qkv_recv.at[kind, t, x])

    def each_outgoing(act):
        for tt in reversed(range(T)):
            for dx in reversed(range(G)):
                for kind in (1, 2, 0):
                    wanted = t > 0 if kind == 0 else t >= 0
                    if dx == 0:
                        wanted = wanted & (t != tt)

                    @pl.when(wanted)
                    def _():
                        act(outgoing(kind, tt, dx))

    each_outgoing(lambda copy: copy.start())
    for kind in (1, 2):
        own(kind).start()

    @pl.when(t > 0)
    def _():
        own(0).start()

    def passed(kind, dc, f, xs):
        return pltpu.make_async_remote_copy(
            src_ref=slot(kind, f, xs), dst_ref=slot(kind, f, xs),
            send_sem=pass_send.at[kind - 1, dc, f, xs], recv_sem=pass_recv.at[kind - 1, dc, f, xs],
            **to(t, x * C + lax.rem(c + dc, C)),
        )

    for copy in loads:
        copy.wait()
    fb[...] = jnp.zeros_like(fb)
    for f in range(T):
        landed(mb.at[f], meta_recv.at[f])
        for b in range(mask_row):
            fb[f : f + 1, b * HD : (b + 1) * HD] = mb[f, b : b + 1, :]
    gb[...] = jnp.dot(
        fb[...], twb[...].astype(jnp.float32),
        precision=lax.Precision.HIGHEST, preferred_element_type=jnp.float32,
    )

    def arrive(f):
        for dx in range(G):
            xs = lax.rem(x + dx, G)
            for kind in (1, 2):
                landed(slot(kind, f, xs), qkv_recv.at[kind, f, xs])
                for dc in range(1, C):
                    passed(kind, dc, f, xs).start()
        for xs in range(G):
            if f > 0:
                landed(slot(0, f, xs), qkv_recv.at[0, f, xs])
            for kind in (1, 2):
                for dc in range(1, C):
                    from_c = xs * C + lax.rem(c + C - dc, C)
                    landed(sources[kind][1].at[f, from_c], pass_recv.at[kind - 1, dc, f, xs])

    def across(r, dx):
        xx = lax.rem(x + dx, G)
        return pltpu.make_async_remote_copy(
            src_ref=ab.at[x, r, c], dst_ref=ab.at[x, r, c],
            send_sem=ax_send.at[r, dx], recv_sem=ax_recv.at[r, dx],
            **to(t, xx * C + c),
        )

    def aside(r, dx, dc):
        xs = lax.rem(x + dx, G)
        return pltpu.make_async_remote_copy(
            src_ref=ab.at[xs, r, c], dst_ref=ab.at[xs, r, c],
            send_sem=ac_send.at[r, dx, dc], recv_sem=ac_recv.at[r, dx, dc],
            **to(t, x * C + lax.rem(c + dc, C)),
        )

    scale = 1.0 / math.sqrt(HD)

    def attend(r):
        f = r + 1
        keys_here = (f + 1) * tokens
        allowed = jnp.concatenate(
            [
                jnp.broadcast_to(mb[f, mask_row + g : mask_row + g + 1, 0:1], (1, tokens))
                for g in range(f + 1)
            ],
            axis=1,
        )
        for j in range(hp):
            cols = slice(j * HD, (j + 1) * HD)
            query = qb[f, :, :, cols].reshape(half, HD)
            key = kb[0 : f + 1, :, :, cols].reshape(keys_here, HD)
            value = vb[0 : f + 1, :, :, cols].reshape(keys_here, HD)
            scores = (
                lax.dot_general(
                    query, key, (((1,), (1,)), ((), ())), preferred_element_type=jnp.float32
                )
                * scale
            )
            scores = jnp.where(allowed > 0.5, scores, -1e30)
            peak = jnp.max(scores, axis=1, keepdims=True)
            lifted = jnp.exp(scores - peak)
            total = jnp.sum(lifted, axis=1, keepdims=True)
            mixed = jnp.dot(
                lifted.astype(jnp.bfloat16), value, preferred_element_type=jnp.float32
            )
            ab[x, r, c, :, cols] = (mixed / total).astype(jnp.bfloat16)
        for dx in range(1, G):
            across(r, dx).start()
        for dc in range(1, C):
            aside(r, 0, dc).start()

    def down(r, p):
        return pltpu.make_async_remote_copy(
            src_ref=down_out.at[r, p], dst_ref=down_in.at[r, p],
            send_sem=dn_send.at[r, p], recv_sem=dn_recv.at[r, p], **to(t - 1, h),
        )

    def up(r, p):
        return pltpu.make_async_remote_copy(
            src_ref=up_out.at[r, p], dst_ref=up_in.at[r, p],
            send_sem=up_send.at[r, p], recv_sem=up_recv.at[r, p], **to(t + 1, h),
        )

    def project(r):
        for dx in range(1, G):
            xs = lax.rem(x + G - dx, G)
            landed(ab.at[xs, r, c], ax_recv.at[r, dx])
            for dc in range(1, C):
                aside(r, G - dx, dc).start()
        for dx in range(G):
            for dc in range(1, C):
                xs, cs = lax.rem(x + dx, G), lax.rem(c + C - dc, C)
                landed(ab.at[xs, r, cs], ac_recv.at[r, dx, dc])
        for p in range(pieces):
            cols = slice(p * nb, (p + 1) * nb)
            gate = gb[r + 1 : r + 2, cols]
            partial = 0.0
            for xs in range(G):
                partial += jnp.dot(
                    ab[xs, r].reshape(tokens, cw),
                    wb[xs * cw : (xs + 1) * cw, cols],
                    preferred_element_type=jnp.float32,
                )
            pb[r, p] = partial * gate

            @pl.when(t == r + 1)
            def _():
                for cs in range(C):
                    for xs in range(G):
                        rows = (cs * G + xs) * tl
                        token = (xs * C + cs) * tl
                        pb[r, p, rows : rows + tl, :] += rb[token : token + tl, cols].astype(
                            jnp.float32
                        )

            @pl.when(t == T - 1)
            def _():
                down_out[r, p] = pb[r, p].astype(jnp.bfloat16)
                down(r, p).start()

            if r > 0:

                @pl.when(t == 0)
                def _():
                    up_out[r, p] = pb[r, p].astype(jnp.bfloat16)
                    up(r, p).start()

    arrive(0)
    for r in range(T - 1):
        arrive(r + 1)
        attend(r)
        project(r)

    for r in reversed(range(2, T - 1)):
        for p in range(pieces):

            @pl.when((t > 0) & (t < r))
            def _():
                landed(up_in.at[r, p], up_recv.at[r, p])
                up_out[r, p] = (pb[r, p] + up_in[r, p].astype(jnp.float32)).astype(jnp.bfloat16)
                up(r, p).start()

    for r in range(T - 2):
        for p in range(pieces):

            @pl.when((t > r) & (t < T - 1))
            def _():
                landed(down_in.at[r, p], dn_recv.at[r, p])
                down_out[r, p] = (pb[r, p] + down_in[r, p].astype(jnp.float32)).astype(
                    jnp.bfloat16
                )
                down(r, p).start()

    for r in range(T - 1):

        @pl.when(t == r)
        def _():
            for p in range(pieces):
                cols = slice(p * nb, (p + 1) * nb)
                landed(down_in.at[r, p], dn_recv.at[r, p])
                if r > 0:
                    landed(up_in.at[r, p], up_recv.at[r, p])
                for cs in range(C):
                    for xs in range(G):
                        rows = slice((cs * G + xs) * tl, (cs * G + xs + 1) * tl)
                        token = (xs * C + cs) * tl
                        total = pb[r, p, rows, :] + down_in[r, p, rows, :].astype(jnp.float32)
                        if r > 0:
                            total += up_in[r, p, rows, :].astype(jnp.float32)
                        out_ref[token : token + tl, cols] = total.astype(out_ref.dtype)

    @pl.when(t == T - 1)
    def _():
        copy = pltpu.make_async_copy(fresh_ref, out_ref, load_sem.at[3])
        copy.start()
        copy.wait()

    for copy in meta_copies:
        copy.wait_send()
    each_outgoing(lambda copy: copy.wait_send())
    for dc in range(1, C):
        for f in range(T):
            for xs in range(G):
                for kind in (1, 2):
                    passed(kind, dc, f, xs).wait_send()
    for r in range(T - 1):
        for dx in range(1, G):
            across(r, dx).wait_send()
        for dx in range(G):
            for dc in range(1, C):
                aside(r, dx, dc).wait_send()
        for p in range(pieces):

            @pl.when(t > r)
            def _():
                down(r, p).wait_send()

            @pl.when(t < r)
            def _():
                up(r, p).wait_send()


def fused(T, H, heads):
    def on_device_fused(
        queries, keys, values, residual, fresh_frame, out_weight, time_weight, noise_steps, frame_mask
    ):
        level_heads = heads // T
        G = math.gcd(level_heads, H)
        C = H // G
        hp = level_heads // G
        tl = queries.shape[1]
        tokens = tl * H
        width = out_weight.shape[1]
        pieces = 2
        nb = width // pieces
        meta_rows = -(-(FREQ // HD + T) // 8) * 8
        meta = jnp.concatenate(
            [
                time_features(noise_steps).reshape(FREQ // HD, HD),
                jnp.broadcast_to(frame_mask[0].astype(jnp.float32)[:, None], (T, HD)),
                jnp.zeros((meta_rows - FREQ // HD - T, HD), jnp.float32),
            ],
            axis=0,
        )
        cw = hp * HD
        bf16, f32 = jnp.bfloat16, jnp.float32
        dma = pltpu.SemaphoreType.DMA
        chunk = (T - 1, pieces, tokens, nb)
        out = pl.pallas_call(
            functools.partial(fused_kernel, T, G, C, hp, pieces),
            out_shape=jax.ShapeDtypeStruct((tokens, width), bf16),
            in_specs=[pl.BlockSpec(memory_space=pl.ANY)] * 8,
            out_specs=pl.BlockSpec(memory_space=pltpu.VMEM),
            scratch_shapes=[
                pltpu.VMEM((T, G, tl, cw), bf16),
                pltpu.VMEM((T, H, tl, cw), bf16),
                pltpu.VMEM((T, H, tl, cw), bf16),
                pltpu.VMEM((G, T - 1, C, G * tl, cw), bf16),
                pltpu.VMEM((T, meta_rows, HD), f32),
                pltpu.VMEM((8, FREQ), f32),
                pltpu.VMEM((8, width), f32),
                pltpu.VMEM(out_weight.shape, bf16),
                pltpu.VMEM(time_weight.shape, bf16),
                pltpu.VMEM((tokens, width), bf16),
                pltpu.VMEM(chunk, f32),
                pltpu.VMEM(chunk, bf16),
                pltpu.VMEM(chunk, bf16),
                pltpu.VMEM(chunk, bf16),
                pltpu.VMEM(chunk, bf16),
                dma((4,)),
                dma((T,)),
                dma((T,)),
                dma((3, T, G)),
                dma((3, T, G)),
                dma((2, C, T, G)),
                dma((2, C, T, G)),
                dma((T - 1, G)),
                dma((T - 1, G)),
                dma((T - 1, G, C)),
                dma((T - 1, G, C)),
                dma((T - 1, pieces)),
                dma((T - 1, pieces)),
                dma((T - 1, pieces)),
                dma((T - 1, pieces)),
            ],
            compiler_params=pltpu.CompilerParams(
                collective_id=0, has_side_effects=True, vmem_limit_bytes=56 * 1024 * 1024
            ),
        )(queries, keys, values, residual, fresh_frame, out_weight, time_weight, meta)
        return out[None]

    return on_device_fused


def solution(mesh):
    placed = (
        P(("groups", "tm"), "head", None),
        P(("groups", "tm"), "head", None),
        P(("groups", "tm"), "head", None),
        P(("groups", "tm"), None, "head"),
        P("groups", "head"),
        P("tm", "head"),
        P(None, "head"),
        P(("groups", "tm")),
        P(("groups", "tm"), None),
    )
    def whole(*args):
        frames, spread = mesh.shape["tm"], mesh.shape["head"]
        heads = args[0].shape[2] // HD
        fits = 1 < frames <= 4 and heads % frames == 0 and args[5].shape[1] % (spread * 2 * HD) == 0
        return jax.shard_map(
            fused(frames, spread, heads) if fits else on_device,
            mesh=mesh,
            in_specs=placed,
            out_specs=P(("groups", "tm"), None, "head"),
            check_vma=False,
        )(*args)

    return whole
```

```python
import functools
import math

import jax
import jax.numpy as jnp
from jax import lax
from jax.experimental import pallas as pl
from jax.experimental.pallas import tpu as pltpu
from jax.sharding import PartitionSpec as P

HD = 128
FREQ = 256
STEPS = 50


def shifted(value, axis, steps):
    count = lax.axis_size(axis)
    leading, last = (max(0, -steps), min(count, count - steps))
    return lax.ppermute(value, axis, [(source, source + steps) for source in range(leading, last)])


def time_features(noise_steps):
    timestep = 1000.0 * (noise_steps.astype(jnp.float32) + 1.0) / STEPS
    half = FREQ // 2
    rates = jnp.exp(-math.log(10000.0) * jnp.arange(half).astype(jnp.float32) / half)
    angles = timestep[:, None] * rates[None, :]
    return jnp.concatenate([jnp.cos(angles), jnp.sin(angles)], axis=1)


def on_device(
    queries, keys, values, residual, fresh_frame, out_weight, time_weight, noise_steps, frame_mask
):
    query_local, key_local, value_local = (
        lax.all_to_all(queries, "head", split_axis=2, concat_axis=1, tiled=True),
        lax.all_to_all(keys, "head", split_axis=2, concat_axis=1, tiled=True),
        lax.all_to_all(values, "head", split_axis=2, concat_axis=1, tiled=True),
    )
    tokens = query_local.shape[1]
    heads_here = query_local.shape[2] // HD
    scale = 1.0 / math.sqrt(HD)
    query_heads = query_local[0].reshape(tokens, heads_here, HD)
    key_value = jnp.stack([key_local[0], value_local[0]], axis=0)
    frame = lax.axis_index("tm")
    frames_total = lax.axis_size("tm")
    window = min(8, frames_total)
    mask_row = frame_mask[0]
    columns = jnp.arange(mask_row.shape[0], dtype=jnp.int32)

    def allowed_at(offset):
        hits = jnp.sum(jnp.where(columns == frame - offset, mask_row, 0))
        return hits > 0

    def absorb(state, block, allowed):
        running_max, weight_sum, accumulated = state
        key_heads = block[0].reshape(tokens, heads_here, HD)
        value_heads = block[1].reshape(tokens, heads_here, HD)
        scores = (
            jnp.einsum("qhd,khd->hqk", query_heads, key_heads, preferred_element_type=jnp.float32)
            * scale
        )
        new_max = jnp.where(allowed, jnp.maximum(running_max, jnp.max(scores, axis=2)), running_max)
        lifted = jnp.where(allowed, jnp.exp(jnp.minimum(scores - new_max[:, :, None], 0.0)), 0.0)
        factor = jnp.exp(running_max - new_max)
        weight_sum = weight_sum * factor + jnp.sum(lifted, axis=2)
        rounded = lifted.astype(jnp.bfloat16)
        accumulated = accumulated * jnp.transpose(factor)[:, :, None] + jnp.einsum(
            "hqk,khd->qhd", rounded, value_heads, preferred_element_type=jnp.float32
        )
        return (new_max, weight_sum, accumulated)

    state = (
        jnp.full((heads_here, tokens), -1e30, jnp.float32),
        jnp.zeros((heads_here, tokens), jnp.float32),
        jnp.zeros((tokens, heads_here, HD), jnp.float32),
    )
    state = absorb(state, key_value, allowed_at(0))
    moving = key_value
    for offset in range(1, window):
        moving = shifted(moving, "tm", 1)
        state = absorb(state, moving, allowed_at(offset))
    running_max, weight_sum, accumulated = state
    attention = (
        (accumulated / jnp.transpose(weight_sum)[:, :, None])
        .reshape(tokens, heads_here * HD)
        .astype(jnp.bfloat16)
    )
    weight_cols = lax.all_gather(out_weight, "tm", axis=0, tiled=True)
    projected = jnp.dot(
        lax.all_gather(attention, "head", axis=1, tiled=True),
        weight_cols,
        preferred_element_type=jnp.float32,
    )
    gate = jnp.dot(
        time_features(noise_steps), time_weight.astype(jnp.float32), precision=lax.Precision.HIGHEST
    )
    updated = (residual[0].astype(jnp.float32) + gate * projected).astype(jnp.bfloat16)
    moved = shifted(updated, "tm", -1)
    rolled = jnp.where(frame == frames_total - 1, fresh_frame, moved)
    return rolled[None]


def fused_kernel(
    T, G, C, hp, pieces,
    q_ref, k_ref, v_ref, res_ref, fresh_ref, w_ref, tw_ref, meta_ref,
    out_ref,
    qb, kb, vb, ab, mb, fb, gb, wb, twb, rb, pb, down_out, down_in, up_out, up_in,
    load_sem, meta_send, meta_recv, qkv_send, qkv_recv, pass_send, pass_recv,
    ax_send, ax_recv, ac_send, ac_recv, dn_send, dn_recv, up_send, up_recv,
):
    t = lax.axis_index("tm")
    h = lax.axis_index("head")
    x = h // C
    c = lax.rem(h, C)
    H = G * C
    tl = q_ref.shape[1]
    cw = hp * HD
    tokens = tl * H
    half = G * tl
    nb = w_ref.shape[1] // pieces
    mask_row = FREQ // HD

    def to(tt, hh):
        return dict(device_id={"tm": tt, "head": hh}, device_id_type=pl.DeviceIdType.MESH)

    def landed(ref, sem):
        pltpu.make_async_copy(ref, ref, sem).wait()

    others = [(dt, dx) for dt in range(T) for dx in reversed(range(G)) if (dt, dx) != (0, 0)]

    loads = [
        pltpu.make_async_copy(w_ref, wb, load_sem.at[0]),
        pltpu.make_async_copy(res_ref.at[0], rb, load_sem.at[1]),
        pltpu.make_async_copy(tw_ref, twb, load_sem.at[2]),
    ]
    for copy in loads:
        copy.start()

    barrier = pltpu.get_barrier_semaphore()
    for dt, dx in others:
        pl.semaphore_signal(
            barrier, inc=1, **to(lax.rem(t + dt, T), lax.rem(x + dx, G) * C + c)
        )
    for dc in range(1, C):
        pl.semaphore_signal(barrier, inc=1, **to(t, x * C + lax.rem(c + dc, C)))
    pl.semaphore_wait(barrier, len(others) + C - 1)

    own_meta = pltpu.make_async_copy(meta_ref, mb.at[t], meta_recv.at[t])
    own_meta.start()
    meta_copies = []
    for dt in range(1, T):
        meta_copies.append(
            pltpu.make_async_remote_copy(
                src_ref=meta_ref, dst_ref=mb.at[t], send_sem=meta_send.at[dt],
                recv_sem=meta_recv.at[t], **to(lax.rem(t + dt, T), h),
            )
        )
        meta_copies[-1].start()

    sources = ((q_ref, qb), (k_ref, kb), (v_ref, vb))

    def slot(kind, f, xs):
        return qb.at[f, xs] if kind == 0 else sources[kind][1].at[f, xs * C + c]

    def block(kind, tt, xx):
        column = pl.multiple_of((tt * G + xx) * cw, HD)
        return sources[kind][0].at[0, :, pl.ds(column, cw)]

    def outgoing(kind, tt, dx):
        xx = lax.rem(x + dx, G)
        return pltpu.make_async_remote_copy(
            src_ref=block(kind, tt, xx), dst_ref=slot(kind, t, x),
            send_sem=qkv_send.at[kind, tt, dx], recv_sem=qkv_recv.at[kind, t, x],
            **to(tt, xx * C + c),
        )

    def own(kind):
        return pltpu.make_async_copy(block(kind, t, x), slot(kind, t, x), qkv_recv.at[kind, t, x])

    def each_outgoing(act):
        for tt in reversed(range(T)):
            for dx in reversed(range(G)):
                for kind in (1, 2, 0):
                    wanted = t > 0 if kind == 0 else t >= 0
                    if dx == 0:
                        wanted = wanted & (t != tt)

                    @pl.when(wanted)
                    def _():
                        act(outgoing(kind, tt, dx))

    each_outgoing(lambda copy: copy.start())
    for kind in (1, 2):
        own(kind).start()

    @pl.when(t > 0)
    def _():
        own(0).start()

    def passed(kind, dc, f, xs):
        return pltpu.make_async_remote_copy(
            src_ref=slot(kind, f, xs), dst_ref=slot(kind, f, xs),
            send_sem=pass_send.at[kind - 1, dc, f, xs], recv_sem=pass_recv.at[kind - 1, dc, f, xs],
            **to(t, x * C + lax.rem(c + dc, C)),
        )

    for copy in loads:
        copy.wait()
    fb[...] = jnp.zeros_like(fb)
    for f in range(T):
        landed(mb.at[f], meta_recv.at[f])
        for b in range(mask_row):
            fb[f : f + 1, b * HD : (b + 1) * HD] = mb[f, b : b + 1, :]
    gb[...] = jnp.dot(
        fb[...], twb[...].astype(jnp.float32),
        precision=lax.Precision.HIGHEST, preferred_element_type=jnp.float32,
    )

    def arrive(f):
        for dx in range(G):
            xs = lax.rem(x + dx, G)
            for kind in (1, 2):
                landed(slot(kind, f, xs), qkv_recv.at[kind, f, xs])
                for dc in range(1, C):
                    passed(kind, dc, f, xs).start()
        for xs in range(G):
            if f > 0:
                landed(slot(0, f, xs), qkv_recv.at[0, f, xs])
            for kind in (1, 2):
                for dc in range(1, C):
                    from_c = xs * C + lax.rem(c + C - dc, C)
                    landed(sources[kind][1].at[f, from_c], pass_recv.at[kind - 1, dc, f, xs])

    def across(r, dx):
        xx = lax.rem(x + dx, G)
        return pltpu.make_async_remote_copy(
            src_ref=ab.at[x, r, c], dst_ref=ab.at[x, r, c],
            send_sem=ax_send.at[r, dx], recv_sem=ax_recv.at[r, dx],
            **to(t, xx * C + c),
        )

    def aside(r, dx, dc):
        xs = lax.rem(x + dx, G)
        return pltpu.make_async_remote_copy(
            src_ref=ab.at[xs, r, c], dst_ref=ab.at[xs, r, c],
            send_sem=ac_send.at[r, dx, dc], recv_sem=ac_recv.at[r, dx, dc],
            **to(t, x * C + lax.rem(c + dc, C)),
        )

    scale = 1.0 / math.sqrt(HD)

    def attend(r):
        f = r + 1
        keys_here = (f + 1) * tokens
        allowed = jnp.concatenate(
            [
                jnp.broadcast_to(mb[f, mask_row + g : mask_row + g + 1, 0:1], (1, tokens))
                for g in range(f + 1)
            ],
            axis=1,
        )
        for j in range(hp):
            cols = slice(j * HD, (j + 1) * HD)
            query = qb[f, :, :, cols].reshape(half, HD)
            key = kb[0 : f + 1, :, :, cols].reshape(keys_here, HD)
            value = vb[0 : f + 1, :, :, cols].reshape(keys_here, HD)
            scores = (
                lax.dot_general(
                    query, key, (((1,), (1,)), ((), ())), preferred_element_type=jnp.float32
                )
                * scale
            )
            scores = jnp.where(allowed > 0.5, scores, -1e30)
            peak = jnp.max(scores, axis=1, keepdims=True)
            lifted = jnp.exp(scores - peak)
            total = jnp.sum(lifted, axis=1, keepdims=True)
            mixed = jnp.dot(
                lifted.astype(jnp.bfloat16), value, preferred_element_type=jnp.float32
            )
            ab[x, r, c, :, cols] = (mixed / total).astype(jnp.bfloat16)
        for dx in range(1, G):
            across(r, dx).start()
        for dc in range(1, C):
            aside(r, 0, dc).start()

    def down(r, p):
        return pltpu.make_async_remote_copy(
            src_ref=down_out.at[r, p], dst_ref=down_in.at[r, p],
            send_sem=dn_send.at[r, p], recv_sem=dn_recv.at[r, p], **to(t - 1, h),
        )

    def up(r, p):
        return pltpu.make_async_remote_copy(
            src_ref=up_out.at[r, p], dst_ref=up_in.at[r, p],
            send_sem=up_send.at[r, p], recv_sem=up_recv.at[r, p], **to(t + 1, h),
        )

    def hand_over(r):
        for dx in range(1, G):
            xs = lax.rem(x + G - dx, G)
            landed(ab.at[xs, r, c], ax_recv.at[r, dx])
            for dc in range(1, C):
                aside(r, G - dx, dc).start()

    def project(r):
        for dx in range(G):
            for dc in range(1, C):
                xs, cs = lax.rem(x + dx, G), lax.rem(c + C - dc, C)
                landed(ab.at[xs, r, cs], ac_recv.at[r, dx, dc])
        for p in range(pieces):
            cols = slice(p * nb, (p + 1) * nb)
            gate = gb[r + 1 : r + 2, cols]
            partial = 0.0
            for xs in range(G):
                partial += jnp.dot(
                    ab[xs, r].reshape(tokens, cw),
                    wb[xs * cw : (xs + 1) * cw, cols],
                    preferred_element_type=jnp.float32,
                )
            pb[r, p] = partial * gate

            @pl.when(t == r + 1)
            def _():
                for cs in range(C):
                    for xs in range(G):
                        rows = (cs * G + xs) * tl
                        token = (xs * C + cs) * tl
                        pb[r, p, rows : rows + tl, :] += rb[token : token + tl, cols].astype(
                            jnp.float32
                        )

            @pl.when(t == T - 1)
            def _():
                down_out[r, p] = pb[r, p].astype(jnp.bfloat16)
                down(r, p).start()

            if r > 0:

                @pl.when(t == 0)
                def _():
                    up_out[r, p] = pb[r, p].astype(jnp.bfloat16)
                    up(r, p).start()

    def relay_up(r):
        for p in range(pieces):

            @pl.when((t > 0) & (t < r))
            def _():
                landed(up_in.at[r, p], up_recv.at[r, p])
                up_out[r, p] = (pb[r, p] + up_in[r, p].astype(jnp.float32)).astype(jnp.bfloat16)
                up(r, p).start()

    def relay_down(r):
        for p in range(pieces):

            @pl.when((t > r) & (t < T - 1))
            def _():
                landed(down_in.at[r, p], dn_recv.at[r, p])
                down_out[r, p] = (pb[r, p] + down_in[r, p].astype(jnp.float32)).astype(
                    jnp.bfloat16
                )
                down(r, p).start()

    arrive(0)
    for r in range(T - 1):
        arrive(r + 1)
        attend(r)
        if r > 0:
            hand_over(r - 1)
            project(r - 1)
    hand_over(T - 2)
    project(T - 2)
    for r in reversed(range(2, T - 1)):
        relay_up(r)
    for r in range(T - 2):
        relay_down(r)

    for r in range(T - 1):

        @pl.when(t == r)
        def _():
            for p in range(pieces):
                cols = slice(p * nb, (p + 1) * nb)
                landed(down_in.at[r, p], dn_recv.at[r, p])
                if r > 0:
                    landed(up_in.at[r, p], up_recv.at[r, p])
                for cs in range(C):
                    for xs in range(G):
                        rows = slice((cs * G + xs) * tl, (cs * G + xs + 1) * tl)
                        token = (xs * C + cs) * tl
                        total = pb[r, p, rows, :] + down_in[r, p, rows, :].astype(jnp.float32)
                        if r > 0:
                            total += up_in[r, p, rows, :].astype(jnp.float32)
                        out_ref[token : token + tl, cols] = total.astype(out_ref.dtype)

    @pl.when(t == T - 1)
    def _():
        copy = pltpu.make_async_copy(fresh_ref, out_ref, load_sem.at[3])
        copy.start()
        copy.wait()

    for copy in meta_copies:
        copy.wait_send()
    each_outgoing(lambda copy: copy.wait_send())
    for dc in range(1, C):
        for f in range(T):
            for xs in range(G):
                for kind in (1, 2):
                    passed(kind, dc, f, xs).wait_send()
    for r in range(T - 1):
        for dx in range(1, G):
            across(r, dx).wait_send()
        for dx in range(G):
            for dc in range(1, C):
                aside(r, dx, dc).wait_send()
        for p in range(pieces):

            @pl.when(t > r)
            def _():
                down(r, p).wait_send()

            @pl.when(t < r)
            def _():
                up(r, p).wait_send()


def fused(T, H, heads):
    def on_device_fused(
        queries, keys, values, residual, fresh_frame, out_weight, time_weight, noise_steps, frame_mask
    ):
        level_heads = heads // T
        G = math.gcd(level_heads, H)
        C = H // G
        hp = level_heads // G
        tl = queries.shape[1]
        tokens = tl * H
        width = out_weight.shape[1]
        pieces = width // (2 * HD)
        nb = width // pieces
        meta_rows = -(-(FREQ // HD + T) // 8) * 8
        meta = jnp.concatenate(
            [
                time_features(noise_steps).reshape(FREQ // HD, HD),
                jnp.broadcast_to(frame_mask[0].astype(jnp.float32)[:, None], (T, HD)),
                jnp.zeros((meta_rows - FREQ // HD - T, HD), jnp.float32),
            ],
            axis=0,
        )
        cw = hp * HD
        bf16, f32 = jnp.bfloat16, jnp.float32
        dma = pltpu.SemaphoreType.DMA
        chunk = (T - 1, pieces, tokens, nb)
        out = pl.pallas_call(
            functools.partial(fused_kernel, T, G, C, hp, pieces),
            out_shape=jax.ShapeDtypeStruct((tokens, width), bf16),
            in_specs=[pl.BlockSpec(memory_space=pl.ANY)] * 8,
            out_specs=pl.BlockSpec(memory_space=pltpu.VMEM),
            scratch_shapes=[
                pltpu.VMEM((T, G, tl, cw), bf16),
                pltpu.VMEM((T, H, tl, cw), bf16),
                pltpu.VMEM((T, H, tl, cw), bf16),
                pltpu.VMEM((G, T - 1, C, G * tl, cw), bf16),
                pltpu.VMEM((T, meta_rows, HD), f32),
                pltpu.VMEM((8, FREQ), f32),
                pltpu.VMEM((8, width), f32),
                pltpu.VMEM(out_weight.shape, bf16),
                pltpu.VMEM(time_weight.shape, bf16),
                pltpu.VMEM((tokens, width), bf16),
                pltpu.VMEM(chunk, f32),
                pltpu.VMEM(chunk, bf16),
                pltpu.VMEM(chunk, bf16),
                pltpu.VMEM(chunk, bf16),
                pltpu.VMEM(chunk, bf16),
                dma((4,)),
                dma((T,)),
                dma((T,)),
                dma((3, T, G)),
                dma((3, T, G)),
                dma((2, C, T, G)),
                dma((2, C, T, G)),
                dma((T - 1, G)),
                dma((T - 1, G)),
                dma((T - 1, G, C)),
                dma((T - 1, G, C)),
                dma((T - 1, pieces)),
                dma((T - 1, pieces)),
                dma((T - 1, pieces)),
                dma((T - 1, pieces)),
            ],
            compiler_params=pltpu.CompilerParams(
                collective_id=0, has_side_effects=True, vmem_limit_bytes=56 * 1024 * 1024
            ),
        )(queries, keys, values, residual, fresh_frame, out_weight, time_weight, meta)
        return out[None]

    return on_device_fused


def solution(mesh):
    placed = (
        P(("groups", "tm"), "head", None),
        P(("groups", "tm"), "head", None),
        P(("groups", "tm"), "head", None),
        P(("groups", "tm"), None, "head"),
        P("groups", "head"),
        P("tm", "head"),
        P(None, "head"),
        P(("groups", "tm")),
        P(("groups", "tm"), None),
    )
    def whole(*args):
        frames, spread = mesh.shape["tm"], mesh.shape["head"]
        heads = args[0].shape[2] // HD
        fits = 1 < frames <= 4 and heads % frames == 0 and args[5].shape[1] % (spread * 2 * HD) == 0
        return jax.shard_map(
            fused(frames, spread, heads) if fits else on_device,
            mesh=mesh,
            in_specs=placed,
            out_specs=P(("groups", "tm"), None, "head"),
            check_vma=False,
        )(*args)

    return whole
```

```python
import functools
import math

import jax
import jax.numpy as jnp
from jax import lax
from jax.experimental import pallas as pl
from jax.experimental.pallas import tpu as pltpu
from jax.sharding import PartitionSpec as P

HD = 128
FREQ = 256
STEPS = 50


def shifted(value, axis, steps):
    count = lax.axis_size(axis)
    leading, last = (max(0, -steps), min(count, count - steps))
    return lax.ppermute(value, axis, [(source, source + steps) for source in range(leading, last)])


def time_features(noise_steps):
    timestep = 1000.0 * (noise_steps.astype(jnp.float32) + 1.0) / STEPS
    half = FREQ // 2
    rates = jnp.exp(-math.log(10000.0) * jnp.arange(half).astype(jnp.float32) / half)
    angles = timestep[:, None] * rates[None, :]
    return jnp.concatenate([jnp.cos(angles), jnp.sin(angles)], axis=1)


def on_device(
    queries, keys, values, residual, fresh_frame, out_weight, time_weight, noise_steps, frame_mask
):
    query_local, key_local, value_local = (
        lax.all_to_all(queries, "head", split_axis=2, concat_axis=1, tiled=True),
        lax.all_to_all(keys, "head", split_axis=2, concat_axis=1, tiled=True),
        lax.all_to_all(values, "head", split_axis=2, concat_axis=1, tiled=True),
    )
    tokens = query_local.shape[1]
    heads_here = query_local.shape[2] // HD
    scale = 1.0 / math.sqrt(HD)
    query_heads = query_local[0].reshape(tokens, heads_here, HD)
    key_value = jnp.stack([key_local[0], value_local[0]], axis=0)
    frame = lax.axis_index("tm")
    frames_total = lax.axis_size("tm")
    window = min(8, frames_total)
    mask_row = frame_mask[0]
    columns = jnp.arange(mask_row.shape[0], dtype=jnp.int32)

    def allowed_at(offset):
        hits = jnp.sum(jnp.where(columns == frame - offset, mask_row, 0))
        return hits > 0

    def absorb(state, block, allowed):
        running_max, weight_sum, accumulated = state
        key_heads = block[0].reshape(tokens, heads_here, HD)
        value_heads = block[1].reshape(tokens, heads_here, HD)
        scores = (
            jnp.einsum("qhd,khd->hqk", query_heads, key_heads, preferred_element_type=jnp.float32)
            * scale
        )
        new_max = jnp.where(allowed, jnp.maximum(running_max, jnp.max(scores, axis=2)), running_max)
        lifted = jnp.where(allowed, jnp.exp(jnp.minimum(scores - new_max[:, :, None], 0.0)), 0.0)
        factor = jnp.exp(running_max - new_max)
        weight_sum = weight_sum * factor + jnp.sum(lifted, axis=2)
        rounded = lifted.astype(jnp.bfloat16)
        accumulated = accumulated * jnp.transpose(factor)[:, :, None] + jnp.einsum(
            "hqk,khd->qhd", rounded, value_heads, preferred_element_type=jnp.float32
        )
        return (new_max, weight_sum, accumulated)

    state = (
        jnp.full((heads_here, tokens), -1e30, jnp.float32),
        jnp.zeros((heads_here, tokens), jnp.float32),
        jnp.zeros((tokens, heads_here, HD), jnp.float32),
    )
    state = absorb(state, key_value, allowed_at(0))
    moving = key_value
    for offset in range(1, window):
        moving = shifted(moving, "tm", 1)
        state = absorb(state, moving, allowed_at(offset))
    running_max, weight_sum, accumulated = state
    attention = (
        (accumulated / jnp.transpose(weight_sum)[:, :, None])
        .reshape(tokens, heads_here * HD)
        .astype(jnp.bfloat16)
    )
    weight_cols = lax.all_gather(out_weight, "tm", axis=0, tiled=True)
    projected = jnp.dot(
        lax.all_gather(attention, "head", axis=1, tiled=True),
        weight_cols,
        preferred_element_type=jnp.float32,
    )
    gate = jnp.dot(
        time_features(noise_steps), time_weight.astype(jnp.float32), precision=lax.Precision.HIGHEST
    )
    updated = (residual[0].astype(jnp.float32) + gate * projected).astype(jnp.bfloat16)
    moved = shifted(updated, "tm", -1)
    rolled = jnp.where(frame == frames_total - 1, fresh_frame, moved)
    return rolled[None]


def fused_kernel(
    T, G, C, hp, pieces, kept, groups,
    q_ref, k_ref, v_ref, res_ref, fresh_ref, w_ref, tw_ref, meta_ref,
    out_ref,
    qb, kb, vb, ab, mb, fb, gb, wb, twb, rb, pb, down_out, down_in, up_out, up_in, ab3, w3,
    load_sem, meta_send, meta_recv, qkv_send, qkv_recv, pass_send, pass_recv,
    ax_send, ax_recv, ac_send, ac_recv, dn_send, dn_recv, up_send, up_recv,
    w_send, w_recv, l_send, l_recv, lx_send, lx_recv, lc_send, lc_recv,
):
    t = lax.axis_index("tm")
    h = lax.axis_index("head")
    x = h // C
    c = lax.rem(h, C)
    H = G * C
    tl = q_ref.shape[1]
    cw = hp * HD
    tokens = tl * H
    half = G * tl
    nb = w_ref.shape[1] // pieces
    mask_row = FREQ // HD

    def to(tt, hh):
        return dict(device_id={"tm": tt, "head": hh}, device_id_type=pl.DeviceIdType.MESH)

    group = lax.axis_index("groups")
    share = w_ref.shape[0] // groups

    def beside(dg):
        return dict(
            device_id={"groups": lax.rem(group + dg, groups)}, device_id_type=pl.DeviceIdType.MESH
        )

    def landed(ref, sem):
        pltpu.make_async_copy(ref, ref, sem).wait()

    others = [(dt, dx) for dt in range(T) for dx in reversed(range(G)) if (dt, dx) != (0, 0)]

    loads = [
        pltpu.make_async_copy(w_ref, wb, load_sem.at[0]),
        pltpu.make_async_copy(res_ref.at[0], rb, load_sem.at[1]),
        pltpu.make_async_copy(tw_ref, twb, load_sem.at[2]),
    ]
    for copy in loads:
        copy.start()

    barrier = pltpu.get_barrier_semaphore()
    for dt, dx in others:
        pl.semaphore_signal(
            barrier, inc=1, **to(lax.rem(t + dt, T), lax.rem(x + dx, G) * C + c)
        )
    for dc in range(1, C):
        pl.semaphore_signal(barrier, inc=1, **to(t, x * C + lax.rem(c + dc, C)))
    for dg in range(1, groups):
        pl.semaphore_signal(barrier, inc=1, **beside(dg))
    pl.semaphore_wait(barrier, len(others) + C - 1 + groups - 1)

    own_meta = pltpu.make_async_copy(meta_ref, mb.at[t], meta_recv.at[t])
    own_meta.start()
    meta_copies = []
    for dt in range(1, T):
        meta_copies.append(
            pltpu.make_async_remote_copy(
                src_ref=meta_ref, dst_ref=mb.at[t], send_sem=meta_send.at[dt],
                recv_sem=meta_recv.at[t], **to(lax.rem(t + dt, T), h),
            )
        )
        meta_copies[-1].start()

    sources = ((q_ref, qb), (k_ref, kb), (v_ref, vb))

    def slot(kind, f, xs):
        return qb.at[f, xs] if kind == 0 else sources[kind][1].at[f, xs * C + c]

    def block(kind, tt, xx):
        column = pl.multiple_of((tt * G + xx) * cw, HD)
        return sources[kind][0].at[0, :, pl.ds(column, cw)]

    def outgoing(kind, dt, dx):
        tt, xx = lax.rem(t + dt, T), lax.rem(x + dx, G)
        return pltpu.make_async_remote_copy(
            src_ref=block(kind, tt, xx), dst_ref=slot(kind, t, x),
            send_sem=qkv_send.at[kind, dt, dx], recv_sem=qkv_recv.at[kind, t, x],
            **to(tt, xx * C + c),
        )

    def own(kind):
        return pltpu.make_async_copy(block(kind, t, x), slot(kind, t, x), qkv_recv.at[kind, t, x])

    def each_outgoing(act):
        for dt, dx in others:
            for kind in (1, 2):
                act(outgoing(kind, dt, dx))

            @pl.when(t > 0)
            def _():
                act(outgoing(0, dt, dx))

    own_rows = pl.ds(group * share, share)

    def lift_weight():
        return pltpu.make_async_remote_copy(
            src_ref=w_ref.at[own_rows, pl.ds(kept * nb, w3.shape[1])], dst_ref=w3.at[own_rows],
            send_sem=w_send.at[0], recv_sem=w_recv.at[0], **to(t - 1, h),
        )

    def trade_weight(dg):
        return pltpu.make_async_remote_copy(
            src_ref=w3.at[own_rows], dst_ref=w3.at[own_rows],
            send_sem=w_send.at[dg], recv_sem=w_recv.at[dg], **beside(dg),
        )

    @pl.when(t == T - 1)
    def _():
        lift_weight().start()

    each_outgoing(lambda copy: copy.start())
    for kind in (1, 2):
        own(kind).start()

    @pl.when(t > 0)
    def _():
        own(0).start()

    def passed(kind, dc, f, xs):
        return pltpu.make_async_remote_copy(
            src_ref=slot(kind, f, xs), dst_ref=slot(kind, f, xs),
            send_sem=pass_send.at[kind - 1, dc, f, xs], recv_sem=pass_recv.at[kind - 1, dc, f, xs],
            **to(t, x * C + lax.rem(c + dc, C)),
        )

    for copy in loads:
        copy.wait()
    fb[...] = jnp.zeros_like(fb)
    for f in range(T):
        landed(mb.at[f], meta_recv.at[f])
        for b in range(mask_row):
            fb[f : f + 1, b * HD : (b + 1) * HD] = mb[f, b : b + 1, :]
    gb[...] = jnp.dot(
        fb[...], twb[...].astype(jnp.float32),
        precision=lax.Precision.HIGHEST, preferred_element_type=jnp.float32,
    )

    def arrive(f):
        for dx in range(G):
            xs = lax.rem(x + dx, G)
            for kind in (1, 2):
                landed(slot(kind, f, xs), qkv_recv.at[kind, f, xs])
                for dc in range(1, C):
                    passed(kind, dc, f, xs).start()
        for xs in range(G):
            if f > 0:
                landed(slot(0, f, xs), qkv_recv.at[0, f, xs])
            for kind in (1, 2):
                for dc in range(1, C):
                    from_c = xs * C + lax.rem(c + C - dc, C)
                    landed(sources[kind][1].at[f, from_c], pass_recv.at[kind - 1, dc, f, xs])

    def across(r, dx):
        xx = lax.rem(x + dx, G)
        return pltpu.make_async_remote_copy(
            src_ref=ab.at[x, r, c], dst_ref=ab.at[x, r, c],
            send_sem=ax_send.at[r, dx], recv_sem=ax_recv.at[r, dx],
            **to(t, xx * C + c),
        )

    def aside(r, dx, dc):
        xs = lax.rem(x + dx, G)
        return pltpu.make_async_remote_copy(
            src_ref=ab.at[xs, r, c], dst_ref=ab.at[xs, r, c],
            send_sem=ac_send.at[r, dx, dc], recv_sem=ac_recv.at[r, dx, dc],
            **to(t, x * C + lax.rem(c + dc, C)),
        )

    scale = 1.0 / math.sqrt(HD)

    def lifted_up(r):
        return pltpu.make_async_remote_copy(
            src_ref=ab.at[x, r, c], dst_ref=ab3.at[x, r, c],
            send_sem=l_send.at[r], recv_sem=l_recv.at[r], **to(t - 1, h),
        )

    def across3(r, dx):
        xx = lax.rem(x + dx, G)
        return pltpu.make_async_remote_copy(
            src_ref=ab3.at[x, r, c], dst_ref=ab3.at[x, r, c],
            send_sem=lx_send.at[r, dx], recv_sem=lx_recv.at[r, dx],
            **to(t, xx * C + c),
        )

    def aside3(r, dx, dc):
        xs = lax.rem(x + dx, G)
        return pltpu.make_async_remote_copy(
            src_ref=ab3.at[xs, r, c], dst_ref=ab3.at[xs, r, c],
            send_sem=lc_send.at[r, dx, dc], recv_sem=lc_recv.at[r, dx, dc],
            **to(t, x * C + lax.rem(c + dc, C)),
        )

    def spread3(r):
        landed(ab3.at[x, r, c], l_recv.at[r])
        for dx in range(1, G):
            across3(r, dx).start()
        for dc in range(1, C):
            aside3(r, 0, dc).start()

    def hand_over3(r):
        for dx in range(1, G):
            xs = lax.rem(x + G - dx, G)
            landed(ab3.at[xs, r, c], lx_recv.at[r, dx])
            for dc in range(1, C):
                aside3(r, G - dx, dc).start()

    def project3(r):
        for dx in range(G):
            for dc in range(1, C):
                xs, cs = lax.rem(x + dx, G), lax.rem(c + C - dc, C)
                landed(ab3.at[xs, r, cs], lc_recv.at[r, dx, dc])
        for p in range(kept, pieces):
            cols = slice((p - kept) * nb, (p - kept + 1) * nb)
            partial = 0.0
            for xs in range(G):
                partial += jnp.dot(
                    ab3[xs, r].reshape(tokens, cw),
                    w3[xs * cw : (xs + 1) * cw, cols],
                    preferred_element_type=jnp.float32,
                )
            pb[r, p] += partial * gb[r + 1 : r + 2, p * nb : (p + 1) * nb]

    def attend(r):
        f = r + 1
        keys_here = (f + 1) * tokens
        allowed = jnp.concatenate(
            [
                jnp.broadcast_to(mb[f, mask_row + g : mask_row + g + 1, 0:1], (1, tokens))
                for g in range(f + 1)
            ],
            axis=1,
        )
        for j in range(hp):
            cols = slice(j * HD, (j + 1) * HD)
            query = qb[f, :, :, cols].reshape(half, HD)
            key = kb[0 : f + 1, :, :, cols].reshape(keys_here, HD)
            value = vb[0 : f + 1, :, :, cols].reshape(keys_here, HD)
            scores = (
                lax.dot_general(
                    query, key, (((1,), (1,)), ((), ())), preferred_element_type=jnp.float32
                )
                * scale
            )
            scores = jnp.where(allowed > 0.5, scores, -1e30)
            peak = jnp.max(scores, axis=1, keepdims=True)
            lifted = jnp.exp(scores - peak)
            total = jnp.sum(lifted, axis=1, keepdims=True)
            mixed = jnp.dot(
                lifted.astype(jnp.bfloat16), value, preferred_element_type=jnp.float32
            )
            ab[x, r, c, :, cols] = (mixed / total).astype(jnp.bfloat16)
        if r < T - 2:

            @pl.when(t == T - 1)
            def _():
                lifted_up(r).start()

        for dx in range(1, G):
            across(r, dx).start()
        for dc in range(1, C):
            aside(r, 0, dc).start()

    def down(r, p):
        return pltpu.make_async_remote_copy(
            src_ref=down_out.at[r, p], dst_ref=down_in.at[r, p],
            send_sem=dn_send.at[r, p], recv_sem=dn_recv.at[r, p], **to(t - 1, h),
        )

    def up(r, p):
        return pltpu.make_async_remote_copy(
            src_ref=up_out.at[r, p], dst_ref=up_in.at[r, p],
            send_sem=up_send.at[r, p], recv_sem=up_recv.at[r, p], **to(t + 1, h),
        )

    def hand_over(r):
        for dx in range(1, G):
            xs = lax.rem(x + G - dx, G)
            landed(ab.at[xs, r, c], ax_recv.at[r, dx])
            for dc in range(1, C):
                aside(r, G - dx, dc).start()

    def project(r):
        for dx in range(G):
            for dc in range(1, C):
                xs, cs = lax.rem(x + dx, G), lax.rem(c + C - dc, C)
                landed(ab.at[xs, r, cs], ac_recv.at[r, dx, dc])
        for p in range(pieces):
            cols = slice(p * nb, (p + 1) * nb)
            gate = gb[r + 1 : r + 2, cols]
            partial = 0.0
            for xs in range(G):
                partial += jnp.dot(
                    ab[xs, r].reshape(tokens, cw),
                    wb[xs * cw : (xs + 1) * cw, cols],
                    preferred_element_type=jnp.float32,
                )
            pb[r, p] = partial * gate

            @pl.when(t == r + 1)
            def _():
                for cs in range(C):
                    for xs in range(G):
                        rows = (cs * G + xs) * tl
                        token = (xs * C + cs) * tl
                        pb[r, p, rows : rows + tl, :] += rb[token : token + tl, cols].astype(
                            jnp.float32
                        )

            if r == T - 2 or p < kept:

                @pl.when(t == T - 1)
                def _():
                    down_out[r, p] = pb[r, p].astype(jnp.bfloat16)
                    down(r, p).start()

            if r > 0:

                @pl.when(t == 0)
                def _():
                    up_out[r, p] = pb[r, p].astype(jnp.bfloat16)
                    up(r, p).start()

    def relay_up(r):
        for p in range(pieces):

            @pl.when((t > 0) & (t < r))
            def _():
                landed(up_in.at[r, p], up_recv.at[r, p])
                up_out[r, p] = (pb[r, p] + up_in[r, p].astype(jnp.float32)).astype(jnp.bfloat16)
                up(r, p).start()

    def relay_down(r):
        for p in range(pieces):

            if p >= kept:

                @pl.when(t == T - 2)
                def _():
                    down_out[r, p] = pb[r, p].astype(jnp.bfloat16)
                    down(r, p).start()

            @pl.when((t > r) & (t < (T - 2 if p >= kept else T - 1)))
            def _():
                landed(down_in.at[r, p], dn_recv.at[r, p])
                down_out[r, p] = (pb[r, p] + down_in[r, p].astype(jnp.float32)).astype(
                    jnp.bfloat16
                )
                down(r, p).start()

    arrive(0)
    for r in range(T - 1):
        arrive(r + 1)
        attend(r)
        if r == 0:

            @pl.when(t == T - 2)
            def _():
                landed(w3.at[own_rows], w_recv.at[0])
                for dg in range(1, groups):
                    trade_weight(dg).start()

        if r > 0:
            hand_over(r - 1)
            project(r - 1)
    @pl.when(t == T - 2)
    def _():
        for r in range(T - 2):
            spread3(r)

    hand_over(T - 2)
    project(T - 2)

    @pl.when(t == T - 2)
    def _():
        for r in range(T - 2):
            hand_over3(r)
        for dg in range(1, groups):
            theirs = pl.ds(lax.rem(group + groups - dg, groups) * share, share)
            landed(w3.at[theirs], w_recv.at[dg])
        for r in range(T - 2):
            project3(r)

    for r in reversed(range(2, T - 1)):
        relay_up(r)
    for r in range(T - 2):
        relay_down(r)

    for r in range(T - 1):

        @pl.when(t == r)
        def _():
            for p in range(pieces):
                cols = slice(p * nb, (p + 1) * nb)
                landed(down_in.at[r, p], dn_recv.at[r, p])
                if r > 0:
                    landed(up_in.at[r, p], up_recv.at[r, p])
                for cs in range(C):
                    for xs in range(G):
                        rows = slice((cs * G + xs) * tl, (cs * G + xs + 1) * tl)
                        token = (xs * C + cs) * tl
                        total = pb[r, p, rows, :] + down_in[r, p, rows, :].astype(jnp.float32)
                        if r > 0:
                            total += up_in[r, p, rows, :].astype(jnp.float32)
                        out_ref[token : token + tl, cols] = total.astype(out_ref.dtype)

    @pl.when(t == T - 1)
    def _():
        copy = pltpu.make_async_copy(fresh_ref, out_ref, load_sem.at[3])
        copy.start()
        copy.wait()

    for copy in meta_copies:
        copy.wait_send()
    each_outgoing(lambda copy: copy.wait_send())

    @pl.when(t == T - 1)
    def _():
        lift_weight().wait_send()
        for r in range(T - 2):
            lifted_up(r).wait_send()

    @pl.when(t == T - 2)
    def _():
        for dg in range(1, groups):
            trade_weight(dg).wait_send()
        for r in range(T - 2):
            for dx in range(1, G):
                across3(r, dx).wait_send()
            for dx in range(G):
                for dc in range(1, C):
                    aside3(r, dx, dc).wait_send()

    for dc in range(1, C):
        for f in range(T):
            for xs in range(G):
                for kind in (1, 2):
                    passed(kind, dc, f, xs).wait_send()
    for r in range(T - 1):
        for dx in range(1, G):
            across(r, dx).wait_send()
        for dx in range(G):
            for dc in range(1, C):
                aside(r, dx, dc).wait_send()
        for p in range(pieces):

            @pl.when((t > r) if r == T - 2 or p < kept else (t > r) & (t < T - 1))
            def _():
                down(r, p).wait_send()

            @pl.when(t < r)
            def _():
                up(r, p).wait_send()


def fused(T, H, heads, groups):
    def on_device_fused(
        queries, keys, values, residual, fresh_frame, out_weight, time_weight, noise_steps, frame_mask
    ):
        level_heads = heads // T
        G = math.gcd(level_heads, H)
        C = H // G
        hp = level_heads // G
        tl = queries.shape[1]
        tokens = tl * H
        width = out_weight.shape[1]
        pieces = width // (2 * HD)
        nb = width // pieces
        kept = 2 * pieces // 5
        meta_rows = -(-(FREQ // HD + T) // 8) * 8
        meta = jnp.concatenate(
            [
                time_features(noise_steps).reshape(FREQ // HD, HD),
                jnp.broadcast_to(frame_mask[0].astype(jnp.float32)[:, None], (T, HD)),
                jnp.zeros((meta_rows - FREQ // HD - T, HD), jnp.float32),
            ],
            axis=0,
        )
        cw = hp * HD
        bf16, f32 = jnp.bfloat16, jnp.float32
        dma = pltpu.SemaphoreType.DMA
        chunk = (T - 1, pieces, tokens, nb)
        out = pl.pallas_call(
            functools.partial(fused_kernel, T, G, C, hp, pieces, kept, groups),
            out_shape=jax.ShapeDtypeStruct((tokens, width), bf16),
            in_specs=[pl.BlockSpec(memory_space=pl.ANY)] * 8,
            out_specs=pl.BlockSpec(memory_space=pltpu.VMEM),
            scratch_shapes=[
                pltpu.VMEM((T, G, tl, cw), bf16),
                pltpu.VMEM((T, H, tl, cw), bf16),
                pltpu.VMEM((T, H, tl, cw), bf16),
                pltpu.VMEM((G, T - 1, C, G * tl, cw), bf16),
                pltpu.VMEM((T, meta_rows, HD), f32),
                pltpu.VMEM((8, FREQ), f32),
                pltpu.VMEM((8, width), f32),
                pltpu.VMEM(out_weight.shape, bf16),
                pltpu.VMEM(time_weight.shape, bf16),
                pltpu.VMEM((tokens, width), bf16),
                pltpu.VMEM(chunk, f32),
                pltpu.VMEM(chunk, bf16),
                pltpu.VMEM(chunk, bf16),
                pltpu.VMEM(chunk, bf16),
                pltpu.VMEM(chunk, bf16),
                pltpu.VMEM((G, T - 1, C, G * tl, cw), bf16),
                pltpu.VMEM((level_heads * HD, (pieces - kept) * nb), bf16),
                dma((4,)),
                dma((T,)),
                dma((T,)),
                dma((3, T, G)),
                dma((3, T, G)),
                dma((2, C, T, G)),
                dma((2, C, T, G)),
                dma((T - 1, G)),
                dma((T - 1, G)),
                dma((T - 1, G, C)),
                dma((T - 1, G, C)),
                dma((T - 1, pieces)),
                dma((T - 1, pieces)),
                dma((T - 1, pieces)),
                dma((T - 1, pieces)),
                dma((groups,)),
                dma((groups,)),
                dma((T - 1,)),
                dma((T - 1,)),
                dma((T - 1, G)),
                dma((T - 1, G)),
                dma((T - 1, G, C)),
                dma((T - 1, G, C)),
            ],
            compiler_params=pltpu.CompilerParams(
                collective_id=0, has_side_effects=True, vmem_limit_bytes=56 * 1024 * 1024
            ),
        )(queries, keys, values, residual, fresh_frame, out_weight, time_weight, meta)
        return out[None]

    return on_device_fused


def solution(mesh):
    placed = (
        P(("groups", "tm"), "head", None),
        P(("groups", "tm"), "head", None),
        P(("groups", "tm"), "head", None),
        P(("groups", "tm"), None, "head"),
        P("groups", "head"),
        P("tm", "head"),
        P(None, "head"),
        P(("groups", "tm")),
        P(("groups", "tm"), None),
    )
    def whole(*args):
        frames, spread = mesh.shape["tm"], mesh.shape["head"]
        heads = args[0].shape[2] // HD
        fits = 2 < frames <= 4 and heads % frames == 0 and args[5].shape[1] % (spread * 2 * HD) == 0
        return jax.shard_map(
            fused(frames, spread, heads, mesh.shape["groups"]) if fits else on_device,
            mesh=mesh,
            in_specs=placed,
            out_specs=P(("groups", "tm"), None, "head"),
            check_vma=False,
        )(*args)

    return whole
```

```python
import functools
import math

import jax
import jax.numpy as jnp
from jax import lax
from jax.experimental import pallas as pl
from jax.experimental.pallas import tpu as pltpu
from jax.sharding import PartitionSpec as P

HD = 128
FREQ = 256
STEPS = 50


def shifted(value, axis, steps):
    count = lax.axis_size(axis)
    leading, last = (max(0, -steps), min(count, count - steps))
    return lax.ppermute(value, axis, [(source, source + steps) for source in range(leading, last)])


def time_features(noise_steps):
    timestep = 1000.0 * (noise_steps.astype(jnp.float32) + 1.0) / STEPS
    half = FREQ // 2
    rates = jnp.exp(-math.log(10000.0) * jnp.arange(half).astype(jnp.float32) / half)
    angles = timestep[:, None] * rates[None, :]
    return jnp.concatenate([jnp.cos(angles), jnp.sin(angles)], axis=1)


def on_device(
    queries, keys, values, residual, fresh_frame, out_weight, time_weight, noise_steps, frame_mask
):
    query_local, key_local, value_local = (
        lax.all_to_all(queries, "head", split_axis=2, concat_axis=1, tiled=True),
        lax.all_to_all(keys, "head", split_axis=2, concat_axis=1, tiled=True),
        lax.all_to_all(values, "head", split_axis=2, concat_axis=1, tiled=True),
    )
    tokens = query_local.shape[1]
    heads_here = query_local.shape[2] // HD
    scale = 1.0 / math.sqrt(HD)
    query_heads = query_local[0].reshape(tokens, heads_here, HD)
    key_value = jnp.stack([key_local[0], value_local[0]], axis=0)
    frame = lax.axis_index("tm")
    frames_total = lax.axis_size("tm")
    window = min(8, frames_total)
    mask_row = frame_mask[0]
    columns = jnp.arange(mask_row.shape[0], dtype=jnp.int32)

    def allowed_at(offset):
        hits = jnp.sum(jnp.where(columns == frame - offset, mask_row, 0))
        return hits > 0

    def absorb(state, block, allowed):
        running_max, weight_sum, accumulated = state
        key_heads = block[0].reshape(tokens, heads_here, HD)
        value_heads = block[1].reshape(tokens, heads_here, HD)
        scores = (
            jnp.einsum("qhd,khd->hqk", query_heads, key_heads, preferred_element_type=jnp.float32)
            * scale
        )
        new_max = jnp.where(allowed, jnp.maximum(running_max, jnp.max(scores, axis=2)), running_max)
        lifted = jnp.where(allowed, jnp.exp(jnp.minimum(scores - new_max[:, :, None], 0.0)), 0.0)
        factor = jnp.exp(running_max - new_max)
        weight_sum = weight_sum * factor + jnp.sum(lifted, axis=2)
        rounded = lifted.astype(jnp.bfloat16)
        accumulated = accumulated * jnp.transpose(factor)[:, :, None] + jnp.einsum(
            "hqk,khd->qhd", rounded, value_heads, preferred_element_type=jnp.float32
        )
        return (new_max, weight_sum, accumulated)

    state = (
        jnp.full((heads_here, tokens), -1e30, jnp.float32),
        jnp.zeros((heads_here, tokens), jnp.float32),
        jnp.zeros((tokens, heads_here, HD), jnp.float32),
    )
    state = absorb(state, key_value, allowed_at(0))
    moving = key_value
    for offset in range(1, window):
        moving = shifted(moving, "tm", 1)
        state = absorb(state, moving, allowed_at(offset))
    running_max, weight_sum, accumulated = state
    attention = (
        (accumulated / jnp.transpose(weight_sum)[:, :, None])
        .reshape(tokens, heads_here * HD)
        .astype(jnp.bfloat16)
    )
    weight_cols = lax.all_gather(out_weight, "tm", axis=0, tiled=True)
    projected = jnp.dot(
        lax.all_gather(attention, "head", axis=1, tiled=True),
        weight_cols,
        preferred_element_type=jnp.float32,
    )
    gate = jnp.dot(
        time_features(noise_steps), time_weight.astype(jnp.float32), precision=lax.Precision.HIGHEST
    )
    updated = (residual[0].astype(jnp.float32) + gate * projected).astype(jnp.bfloat16)
    moved = shifted(updated, "tm", -1)
    rolled = jnp.where(frame == frames_total - 1, fresh_frame, moved)
    return rolled[None]


def fused_kernel(
    T, G, C, hp, pieces, kept, groups,
    q_ref, k_ref, v_ref, res_ref, fresh_ref, w_ref, tw_ref, meta_ref,
    out_ref,
    qb, kb, vb, ab, mb, fb, gb, wb, twb, rb, pb, down_out, down_in, up_out, up_in, ab3, w3,
    load_sem, meta_send, meta_recv, qkv_send, qkv_recv, pass_send, pass_recv,
    ax_send, ax_recv, ac_send, ac_recv, dn_send, dn_recv, up_send, up_recv,
    w_send, w_recv, l_send, l_recv, lx_send, lx_recv, lc_send, lc_recv,
):
    t = lax.axis_index("tm")
    h = lax.axis_index("head")
    x = h // C
    c = lax.rem(h, C)
    H = G * C
    tl = q_ref.shape[1]
    cw = hp * HD
    tokens = tl * H
    half = G * tl
    nb = w_ref.shape[1] // pieces
    mask_row = FREQ // HD

    def to(tt, hh):
        return dict(device_id={"tm": tt, "head": hh}, device_id_type=pl.DeviceIdType.MESH)

    group = lax.axis_index("groups")
    share = w_ref.shape[0] // groups

    def beside(dg):
        return dict(
            device_id={"groups": lax.rem(group + dg, groups)}, device_id_type=pl.DeviceIdType.MESH
        )

    def landed(ref, sem):
        pltpu.make_async_copy(ref, ref, sem).wait()

    others = [(dt, dx) for dt in range(T) for dx in reversed(range(G)) if (dt, dx) != (0, 0)]

    loads = [
        pltpu.make_async_copy(w_ref, wb, load_sem.at[0]),
        pltpu.make_async_copy(res_ref.at[0], rb, load_sem.at[1]),
        pltpu.make_async_copy(tw_ref, twb, load_sem.at[2]),
    ]
    for copy in loads:
        copy.start()

    barrier = pltpu.get_barrier_semaphore()
    for dt, dx in others:
        pl.semaphore_signal(
            barrier, inc=1, **to(lax.rem(t + dt, T), lax.rem(x + dx, G) * C + c)
        )
    for dc in range(1, C):
        pl.semaphore_signal(barrier, inc=1, **to(t, x * C + lax.rem(c + dc, C)))
    for dg in range(1, groups):
        pl.semaphore_signal(barrier, inc=1, **beside(dg))
    pl.semaphore_wait(barrier, len(others) + C - 1 + groups - 1)

    own_meta = pltpu.make_async_copy(meta_ref, mb.at[t], meta_recv.at[t])
    own_meta.start()
    meta_copies = []
    for dt in range(1, T):
        meta_copies.append(
            pltpu.make_async_remote_copy(
                src_ref=meta_ref, dst_ref=mb.at[t], send_sem=meta_send.at[dt],
                recv_sem=meta_recv.at[t], **to(lax.rem(t + dt, T), h),
            )
        )
        meta_copies[-1].start()

    sources = ((q_ref, qb), (k_ref, kb), (v_ref, vb))

    def slot(kind, f, xs):
        return qb.at[f, xs] if kind == 0 else sources[kind][1].at[f, xs * C + c]

    def block(kind, tt, xx):
        column = pl.multiple_of((tt * G + xx) * cw, HD)
        return sources[kind][0].at[0, :, pl.ds(column, cw)]

    def outgoing(kind, dt, dx):
        tt, xx = lax.rem(t + dt, T), lax.rem(x + dx, G)
        return pltpu.make_async_remote_copy(
            src_ref=block(kind, tt, xx), dst_ref=slot(kind, t, x),
            send_sem=qkv_send.at[kind, dt, dx], recv_sem=qkv_recv.at[kind, t, x],
            **to(tt, xx * C + c),
        )

    def own(kind):
        return pltpu.make_async_copy(block(kind, t, x), slot(kind, t, x), qkv_recv.at[kind, t, x])

    def each_outgoing(act):
        for dt, dx in others:
            for kind in (1, 2):
                act(outgoing(kind, dt, dx))

            @pl.when(t > 0)
            def _():
                act(outgoing(0, dt, dx))

    own_rows = pl.ds(group * share, share)

    def lift_weight():
        return pltpu.make_async_remote_copy(
            src_ref=w_ref.at[own_rows, pl.ds(kept * nb, w3.shape[1])], dst_ref=w3.at[own_rows],
            send_sem=w_send.at[0], recv_sem=w_recv.at[0], **to(t - 1, h),
        )

    def trade_weight(dg):
        return pltpu.make_async_remote_copy(
            src_ref=w3.at[own_rows], dst_ref=w3.at[own_rows],
            send_sem=w_send.at[dg], recv_sem=w_recv.at[dg], **beside(dg),
        )

    @pl.when(t == T - 1)
    def _():
        lift_weight().start()

    each_outgoing(lambda copy: copy.start())
    for kind in (1, 2):
        own(kind).start()

    @pl.when(t > 0)
    def _():
        own(0).start()

    def passed(kind, dc, f, xs):
        return pltpu.make_async_remote_copy(
            src_ref=slot(kind, f, xs), dst_ref=slot(kind, f, xs),
            send_sem=pass_send.at[kind - 1, dc, f, xs], recv_sem=pass_recv.at[kind - 1, dc, f, xs],
            **to(t, x * C + lax.rem(c + dc, C)),
        )

    for copy in loads:
        copy.wait()
    fb[...] = jnp.zeros_like(fb)
    for f in range(T):
        landed(mb.at[f], meta_recv.at[f])
        for b in range(mask_row):
            fb[f : f + 1, b * HD : (b + 1) * HD] = mb[f, b : b + 1, :]
    gb[...] = jnp.dot(
        fb[...], twb[...].astype(jnp.float32),
        precision=lax.Precision.HIGHEST, preferred_element_type=jnp.float32,
    )

    def arrive(f):
        for dx in range(G):
            xs = lax.rem(x + dx, G)
            for kind in (1, 2):
                landed(slot(kind, f, xs), qkv_recv.at[kind, f, xs])
                for dc in range(1, C):
                    passed(kind, dc, f, xs).start()
        for xs in range(G):
            if f > 0:
                landed(slot(0, f, xs), qkv_recv.at[0, f, xs])
            for kind in (1, 2):
                for dc in range(1, C):
                    from_c = xs * C + lax.rem(c + C - dc, C)
                    landed(sources[kind][1].at[f, from_c], pass_recv.at[kind - 1, dc, f, xs])

    def across(r, dx):
        xx = lax.rem(x + dx, G)
        return pltpu.make_async_remote_copy(
            src_ref=ab.at[x, r, c], dst_ref=ab.at[x, r, c],
            send_sem=ax_send.at[r, dx], recv_sem=ax_recv.at[r, dx],
            **to(t, xx * C + c),
        )

    def aside(r, dx, dc):
        xs = lax.rem(x + dx, G)
        return pltpu.make_async_remote_copy(
            src_ref=ab.at[xs, r, c], dst_ref=ab.at[xs, r, c],
            send_sem=ac_send.at[r, dx, dc], recv_sem=ac_recv.at[r, dx, dc],
            **to(t, x * C + lax.rem(c + dc, C)),
        )

    scale = 1.0 / math.sqrt(HD)

    def lifted_up(r):
        return pltpu.make_async_remote_copy(
            src_ref=ab.at[x, r, c], dst_ref=ab3.at[x, r, c],
            send_sem=l_send.at[r], recv_sem=l_recv.at[r], **to(t - 1, h),
        )

    def across3(r, dx):
        xx = lax.rem(x + dx, G)
        return pltpu.make_async_remote_copy(
            src_ref=ab3.at[x, r, c], dst_ref=ab3.at[x, r, c],
            send_sem=lx_send.at[r, dx], recv_sem=lx_recv.at[r, dx],
            **to(t, xx * C + c),
        )

    def aside3(r, dx, dc):
        xs = lax.rem(x + dx, G)
        return pltpu.make_async_remote_copy(
            src_ref=ab3.at[xs, r, c], dst_ref=ab3.at[xs, r, c],
            send_sem=lc_send.at[r, dx, dc], recv_sem=lc_recv.at[r, dx, dc],
            **to(t, x * C + lax.rem(c + dc, C)),
        )

    def spread3(r):
        landed(ab3.at[x, r, c], l_recv.at[r])
        for dx in range(1, G):
            across3(r, dx).start()
        for dc in range(1, C):
            aside3(r, 0, dc).start()

    def hand_over3(r):
        for dx in range(1, G):
            xs = lax.rem(x + G - dx, G)
            landed(ab3.at[xs, r, c], lx_recv.at[r, dx])
            for dc in range(1, C):
                aside3(r, G - dx, dc).start()

    def project3(r):
        for dx in range(G):
            for dc in range(1, C):
                xs, cs = lax.rem(x + dx, G), lax.rem(c + C - dc, C)
                landed(ab3.at[xs, r, cs], lc_recv.at[r, dx, dc])
        for p in range(kept, pieces):
            cols = slice((p - kept) * nb, (p - kept + 1) * nb)
            partial = 0.0
            for xs in range(G):
                partial += jnp.dot(
                    ab3[xs, r].reshape(tokens, cw),
                    w3[xs * cw : (xs + 1) * cw, cols],
                    preferred_element_type=jnp.float32,
                )
            pb[r, p] += partial * gb[r + 1 : r + 2, p * nb : (p + 1) * nb]

    def attend(r):
        f = r + 1
        keys_here = (f + 1) * tokens
        allowed = jnp.concatenate(
            [
                jnp.broadcast_to(mb[f, mask_row + g : mask_row + g + 1, 0:1], (1, tokens))
                for g in range(f + 1)
            ],
            axis=1,
        )
        for j in range(hp):
            cols = slice(j * HD, (j + 1) * HD)
            query = qb[f, :, :, cols].reshape(half, HD)
            key = kb[0 : f + 1, :, :, cols].reshape(keys_here, HD)
            value = vb[0 : f + 1, :, :, cols].reshape(keys_here, HD)
            scores = (
                lax.dot_general(
                    query, key, (((1,), (1,)), ((), ())), preferred_element_type=jnp.float32
                )
                * scale
            )
            scores = jnp.where(allowed > 0.5, scores, -1e30)
            peak = jnp.max(scores, axis=1, keepdims=True)
            lifted = jnp.exp(scores - peak)
            total = jnp.sum(lifted, axis=1, keepdims=True)
            mixed = jnp.dot(
                lifted.astype(jnp.bfloat16), value, preferred_element_type=jnp.float32
            )
            ab[x, r, c, :, cols] = (mixed / total).astype(jnp.bfloat16)
        if r < T - 2:

            @pl.when(t == T - 1)
            def _():
                lifted_up(r).start()

        for dx in range(1, G):
            across(r, dx).start()
        for dc in range(1, C):
            aside(r, 0, dc).start()

    def down(r, p):
        return pltpu.make_async_remote_copy(
            src_ref=down_out.at[r, p], dst_ref=down_in.at[r, p],
            send_sem=dn_send.at[r, p], recv_sem=dn_recv.at[r, p], **to(t - 1, h),
        )

    def up(r, p):
        return pltpu.make_async_remote_copy(
            src_ref=up_out.at[r, p], dst_ref=up_in.at[r, p],
            send_sem=up_send.at[r, p], recv_sem=up_recv.at[r, p], **to(t + 1, h),
        )

    def hand_over(r):
        for dx in range(1, G):
            xs = lax.rem(x + G - dx, G)
            landed(ab.at[xs, r, c], ax_recv.at[r, dx])
            for dc in range(1, C):
                aside(r, G - dx, dc).start()

    def project(r):
        for dx in range(G):
            for dc in range(1, C):
                xs, cs = lax.rem(x + dx, G), lax.rem(c + C - dc, C)
                landed(ab.at[xs, r, cs], ac_recv.at[r, dx, dc])
        for p in range(pieces):
            cols = slice(p * nb, (p + 1) * nb)
            gate = gb[r + 1 : r + 2, cols]
            partial = 0.0
            for xs in range(G):
                partial += jnp.dot(
                    ab[xs, r].reshape(tokens, cw),
                    wb[xs * cw : (xs + 1) * cw, cols],
                    preferred_element_type=jnp.float32,
                )
            pb[r, p] = partial * gate

            @pl.when(t == r + 1)
            def _():
                for cs in range(C):
                    for xs in range(G):
                        rows = (cs * G + xs) * tl
                        token = (xs * C + cs) * tl
                        pb[r, p, rows : rows + tl, :] += rb[token : token + tl, cols].astype(
                            jnp.float32
                        )

            if r == T - 2 or p < kept:

                @pl.when(t == T - 1)
                def _():
                    down_out[r, p] = pb[r, p].astype(jnp.bfloat16)
                    down(r, p).start()

            if r > 0:

                @pl.when(t == 0)
                def _():
                    up_out[r, p] = pb[r, p].astype(jnp.bfloat16)
                    up(r, p).start()

    def relay_up(r):
        for p in range(pieces):

            @pl.when((t > 0) & (t < r))
            def _():
                landed(up_in.at[r, p], up_recv.at[r, p])
                up_out[r, p] = (pb[r, p] + up_in[r, p].astype(jnp.float32)).astype(jnp.bfloat16)
                up(r, p).start()

    def relay_down(r):
        for p in range(pieces):

            if p >= kept:

                @pl.when(t == T - 2)
                def _():
                    down_out[r, p] = pb[r, p].astype(jnp.bfloat16)
                    down(r, p).start()

            @pl.when((t > r) & (t < (T - 2 if p >= kept else T - 1)))
            def _():
                landed(down_in.at[r, p], dn_recv.at[r, p])
                down_out[r, p] = (pb[r, p] + down_in[r, p].astype(jnp.float32)).astype(
                    jnp.bfloat16
                )
                down(r, p).start()

    arrive(0)
    for r in range(T - 1):
        arrive(r + 1)
        attend(r)
        if r == 0:

            @pl.when(t == T - 2)
            def _():
                landed(w3.at[own_rows], w_recv.at[0])
                for dg in range(1, groups):
                    trade_weight(dg).start()

        if r > 0:
            hand_over(r - 1)
            project(r - 1)
    @pl.when(t == T - 2)
    def _():
        for r in range(T - 2):
            spread3(r)

    hand_over(T - 2)
    project(T - 2)

    @pl.when(t == T - 2)
    def _():
        for r in range(T - 2):
            hand_over3(r)
        for dg in range(1, groups):
            theirs = pl.ds(lax.rem(group + groups - dg, groups) * share, share)
            landed(w3.at[theirs], w_recv.at[dg])
        project3(0)

    relay_down(0)

    @pl.when(t == T - 2)
    def _():
        for r in range(1, T - 2):
            project3(r)

    for r in reversed(range(2, T - 1)):
        relay_up(r)
    for r in range(1, T - 2):
        relay_down(r)

    for r in range(T - 1):

        @pl.when(t == r)
        def _():
            for p in range(pieces):
                cols = slice(p * nb, (p + 1) * nb)
                landed(down_in.at[r, p], dn_recv.at[r, p])
                if r > 0:
                    landed(up_in.at[r, p], up_recv.at[r, p])
                for cs in range(C):
                    for xs in range(G):
                        rows = slice((cs * G + xs) * tl, (cs * G + xs + 1) * tl)
                        token = (xs * C + cs) * tl
                        total = pb[r, p, rows, :] + down_in[r, p, rows, :].astype(jnp.float32)
                        if r > 0:
                            total += up_in[r, p, rows, :].astype(jnp.float32)
                        out_ref[token : token + tl, cols] = total.astype(out_ref.dtype)

    @pl.when(t == T - 1)
    def _():
        copy = pltpu.make_async_copy(fresh_ref, out_ref, load_sem.at[3])
        copy.start()
        copy.wait()

    for copy in meta_copies:
        copy.wait_send()
    each_outgoing(lambda copy: copy.wait_send())

    @pl.when(t == T - 1)
    def _():
        lift_weight().wait_send()
        for r in range(T - 2):
            lifted_up(r).wait_send()

    @pl.when(t == T - 2)
    def _():
        for dg in range(1, groups):
            trade_weight(dg).wait_send()
        for r in range(T - 2):
            for dx in range(1, G):
                across3(r, dx).wait_send()
            for dx in range(G):
                for dc in range(1, C):
                    aside3(r, dx, dc).wait_send()

    for dc in range(1, C):
        for f in range(T):
            for xs in range(G):
                for kind in (1, 2):
                    passed(kind, dc, f, xs).wait_send()
    for r in range(T - 1):
        for dx in range(1, G):
            across(r, dx).wait_send()
        for dx in range(G):
            for dc in range(1, C):
                aside(r, dx, dc).wait_send()
        for p in range(pieces):

            @pl.when((t > r) if r == T - 2 or p < kept else (t > r) & (t < T - 1))
            def _():
                down(r, p).wait_send()

            @pl.when(t < r)
            def _():
                up(r, p).wait_send()


def fused(T, H, heads, groups):
    def on_device_fused(
        queries, keys, values, residual, fresh_frame, out_weight, time_weight, noise_steps, frame_mask
    ):
        level_heads = heads // T
        G = math.gcd(level_heads, H)
        C = H // G
        hp = level_heads // G
        tl = queries.shape[1]
        tokens = tl * H
        width = out_weight.shape[1]
        pieces = width // (2 * HD)
        nb = width // pieces
        kept = 2 * pieces // 5
        meta_rows = -(-(FREQ // HD + T) // 8) * 8
        meta = jnp.concatenate(
            [
                time_features(noise_steps).reshape(FREQ // HD, HD),
                jnp.broadcast_to(frame_mask[0].astype(jnp.float32)[:, None], (T, HD)),
                jnp.zeros((meta_rows - FREQ // HD - T, HD), jnp.float32),
            ],
            axis=0,
        )
        cw = hp * HD
        bf16, f32 = jnp.bfloat16, jnp.float32
        dma = pltpu.SemaphoreType.DMA
        chunk = (T - 1, pieces, tokens, nb)
        out = pl.pallas_call(
            functools.partial(fused_kernel, T, G, C, hp, pieces, kept, groups),
            out_shape=jax.ShapeDtypeStruct((tokens, width), bf16),
            in_specs=[pl.BlockSpec(memory_space=pl.ANY)] * 8,
            out_specs=pl.BlockSpec(memory_space=pltpu.VMEM),
            scratch_shapes=[
                pltpu.VMEM((T, G, tl, cw), bf16),
                pltpu.VMEM((T, H, tl, cw), bf16),
                pltpu.VMEM((T, H, tl, cw), bf16),
                pltpu.VMEM((G, T - 1, C, G * tl, cw), bf16),
                pltpu.VMEM((T, meta_rows, HD), f32),
                pltpu.VMEM((8, FREQ), f32),
                pltpu.VMEM((8, width), f32),
                pltpu.VMEM(out_weight.shape, bf16),
                pltpu.VMEM(time_weight.shape, bf16),
                pltpu.VMEM((tokens, width), bf16),
                pltpu.VMEM(chunk, f32),
                pltpu.VMEM(chunk, bf16),
                pltpu.VMEM(chunk, bf16),
                pltpu.VMEM(chunk, bf16),
                pltpu.VMEM(chunk, bf16),
                pltpu.VMEM((G, T - 1, C, G * tl, cw), bf16),
                pltpu.VMEM((level_heads * HD, (pieces - kept) * nb), bf16),
                dma((4,)),
                dma((T,)),
                dma((T,)),
                dma((3, T, G)),
                dma((3, T, G)),
                dma((2, C, T, G)),
                dma((2, C, T, G)),
                dma((T - 1, G)),
                dma((T - 1, G)),
                dma((T - 1, G, C)),
                dma((T - 1, G, C)),
                dma((T - 1, pieces)),
                dma((T - 1, pieces)),
                dma((T - 1, pieces)),
                dma((T - 1, pieces)),
                dma((groups,)),
                dma((groups,)),
                dma((T - 1,)),
                dma((T - 1,)),
                dma((T - 1, G)),
                dma((T - 1, G)),
                dma((T - 1, G, C)),
                dma((T - 1, G, C)),
            ],
            compiler_params=pltpu.CompilerParams(
                collective_id=0, has_side_effects=True, vmem_limit_bytes=56 * 1024 * 1024
            ),
        )(queries, keys, values, residual, fresh_frame, out_weight, time_weight, meta)
        return out[None]

    return on_device_fused


def solution(mesh):
    placed = (
        P(("groups", "tm"), "head", None),
        P(("groups", "tm"), "head", None),
        P(("groups", "tm"), "head", None),
        P(("groups", "tm"), None, "head"),
        P("groups", "head"),
        P("tm", "head"),
        P(None, "head"),
        P(("groups", "tm")),
        P(("groups", "tm"), None),
    )
    def whole(*args):
        frames, spread = mesh.shape["tm"], mesh.shape["head"]
        heads = args[0].shape[2] // HD
        fits = 2 < frames <= 4 and heads % frames == 0 and args[5].shape[1] % (spread * 2 * HD) == 0
        return jax.shard_map(
            fused(frames, spread, heads, mesh.shape["groups"]) if fits else on_device,
            mesh=mesh,
            in_specs=placed,
            out_specs=P(("groups", "tm"), None, "head"),
            check_vma=False,
        )(*args)

    return whole
```
